128 devices in a mesh: segment: 4 (over x), dom: 32 (over y, z, core).
Axes of the slice: x: 4, y: 4, z: 4, core: 2. Of those that a mesh axis runs over, the one named last changes fastest.
Arguments:
- features: bfloat16 [4, 16384, 512], P(None, 'dom'), may hold values from -6 to 6
- send_rows: int32 [4, 32, 32, 128], P(None, 'dom'), may hold values from 0 to 511
- send_len: int32 [4, 32, 32], P(None, 'dom'), may hold values from 0 to 128, as said below
- tile_src: int32 [4, 128, 4], P(None, 'dom'), may hold values from 0 to 35
- tile_count: int32 [4, 128], P(None, 'dom'), may hold values from 1 to 4, as said below
- tile_val: bfloat16 [4, 128, 4, 128, 128], P(None, 'dom'), may hold values from -0.25 to 0.25
- w_self: bfloat16 [4, 512, 512], P('segment'), may hold values from -0.25 to 0.25
- w_neigh: bfloat16 [4, 512, 512], P('segment'), may hold values from -0.25 to 0.25
- gain: bfloat16 [4, 512], P('segment'), may hold values from 0.25 to 1.75
- bias: bfloat16 [4, 512], P('segment'), may hold values from -3 to 3
Outputs:
- acts: bfloat16 [4, 4, 16384, 512], P('segment', None, 'dom')
The draws below stay inside these ranges and needn't reach their ends.
Inputs may be any that keep to these rules, and one draw needn't show every extreme that they name: `send_len`: A partition sends nothing to itself; in every span each partition sends a full block of 128 rows to one other partition. `tile_count`: in every span one partition has 4 live tiles in each of its blocks.
All inputs are finite; a program needn't handle non-finite values.
Results may differ from the reference program's by a relative error of at most 0.0065.
Values may be sent and summed in bfloat16 or wider, within the bound.
A program may use at most 64 MiB of HBM per device.

```python
import jax
import jax.numpy as jnp
from jax import lax

D = 512
TILE = 128
NB = 4
K = 4
SPANS = 4
LAYERS = 4
NODES = 16384
N_DOM = 32


def draw_send_len(key, part):
    first_key, second_key = jax.random.split(key)
    lengths = jax.random.randint(first_key, (SPANS, N_DOM, N_DOM), 0, TILE + 1)
    offset = jax.random.randint(second_key, (SPANS, N_DOM, 1), 1, N_DOM)
    sender = lax.broadcasted_iota(jnp.int32, (SPANS, N_DOM, N_DOM), 1)
    target = lax.broadcasted_iota(jnp.int32, (SPANS, N_DOM, N_DOM), 2)
    full_peer = (sender + offset) % N_DOM
    lengths = jnp.where(target == full_peer, TILE, lengths)
    return jnp.where(target == sender, 0, lengths).astype(jnp.int32)


def draw_tile_count(key, part):
    first_key, second_key, third_key = jax.random.split(key, 3)
    load_level = jax.random.randint(first_key, (SPANS, N_DOM, 1), 1, K + 1)
    drawn_raw = jax.random.randint(second_key, (SPANS, N_DOM, NB), 0, K)
    counts = 1 + drawn_raw % load_level
    busy_part = jax.random.randint(third_key, (SPANS, 1, 1), 0, N_DOM)
    partition = lax.broadcasted_iota(jnp.int32, (SPANS, N_DOM, NB), 1)
    counts = jnp.where(partition == busy_part, K, counts)
    return counts.reshape(SPANS, N_DOM * NB).astype(jnp.int32)


def with_ends(array, own_key, smallest, largest):
    dims = array.shape
    index_at = [jax.random.randint(jax.random.fold_in(own_key, axis), (), 0, dims[axis]) for axis in range(len(dims))]
    array = array.at[tuple(index_at)].set(smallest)
    longest = dims.index(max(dims))
    index_at[longest] = (index_at[longest] + 1) % dims[longest]
    return array.at[tuple(index_at)].set(largest)


def block_levels(key, dims, shards, smallest, largest):
    level = 1.0
    for dim, shards_of in shards:
        heights = jax.random.uniform(jax.random.fold_in(jax.random.fold_in(key, 6), dim), (shards_of,), jnp.float32, smallest / len(shards), largest / len(shards))
        level = level * jnp.repeat(jnp.exp(heights), dims[dim] // shards_of).reshape((-1,) + (1,) * (len(dims) - 1 - dim))
    return level


def bell_draw(rng, dims, scale, most, cuts=(), dtype=jnp.bfloat16):
    level = block_levels(rng, dims, cuts, -0.22, 0.18) if cuts else 1.0
    result = jax.random.normal(rng, dims, jnp.float32) * scale * level
    return jnp.minimum(jnp.maximum(result, -most), most).astype(dtype)


def setup_inputs(seed: int = 0) -> dict:
    arg_keys = jax.random.split(jax.random.key(seed), 11)
    features = bell_draw(arg_keys[0], (SPANS, NODES, D), 1.0, 6.0, ((1, 32),))
    send_rows = with_ends(jax.random.randint(arg_keys[1], (SPANS, N_DOM, N_DOM, TILE), 0, NB * TILE), jax.random.fold_in(arg_keys[1], 1), 0, (NB * TILE) - 1).astype(jnp.int32)
    send_len = draw_send_len(jax.random.fold_in(arg_keys[10], 71), 0)
    tile_src = with_ends(jax.random.randint(arg_keys[3], (SPANS, NODES // TILE, K), 0, NB + N_DOM), jax.random.fold_in(arg_keys[3], 1), 0, (NB + N_DOM) - 1).astype(jnp.int32)
    tile_count = draw_tile_count(jax.random.fold_in(arg_keys[10], 71), 0)
    tile_val = bell_draw(arg_keys[5], (SPANS, NODES // TILE, K, TILE, TILE), (TILE * K) ** -0.5, 0.25, ((1, 32),))
    w_self = bell_draw(arg_keys[6], (LAYERS, D, D), D ** -0.5, 0.25, ((0, 4),))
    w_neigh = bell_draw(arg_keys[7], (LAYERS, D, D), D ** -0.5, 0.25, ((0, 4),))
    gain = jnp.clip(1.0 + 0.15 * jax.random.normal(arg_keys[8], (LAYERS, D), jnp.float32), 0.25, 1.75).astype(jnp.bfloat16)
    bias = bell_draw(arg_keys[9], (LAYERS, D), 0.5, 3.0, ((0, 4),))
    return dict(features=features, send_rows=send_rows, send_len=send_len, tile_src=tile_src, tile_count=tile_count, tile_val=tile_val, w_self=w_self, w_neigh=w_neigh, gain=gain, bias=bias)


norm_eps = 1e-05

def take_rows(part_rows, part_list):
    return jnp.take(part_rows, part_list.reshape(-1), axis=0)

def part_sum(packed):
    part_sources, part_src, part_count, part_val = packed
    chosen = jnp.take(part_sources, part_src.reshape(-1), axis=0).reshape(NB, K, TILE, D).astype(jnp.float32)
    keep_tile = lax.broadcasted_iota(jnp.int32, (NB, K), 1) < part_count[:, None]
    coeffs = jnp.where(keep_tile[:, :, None, None], part_val.astype(jnp.float32), jnp.zeros((NB, K, TILE, TILE), jnp.float32))
    return jnp.einsum('bkij,bkjd->bid', coeffs, chosen)

def sage_layer(hidden, rows_c, len_c, src_c, count_c, val_c, w_one, w_two, gain_one, bias_one):
    owned = hidden.reshape(N_DOM, NB * TILE, D)
    picked = jax.vmap(take_rows)(owned, rows_c).reshape(N_DOM, N_DOM, TILE, D)
    row_live = lax.broadcasted_iota(jnp.int32, (N_DOM, N_DOM, TILE), 2) < len_c[:, :, None]
    halo = jnp.where(row_live[:, :, :, None], picked, jnp.zeros_like(picked))
    arriving = jnp.transpose(halo, (1, 0, 2, 3))
    sources = jnp.concatenate([owned.reshape(N_DOM, NB, TILE, D), arriving], axis=1)
    summed = lax.map(part_sum, (sources, src_c.reshape(N_DOM, NB, K), count_c.reshape(N_DOM, NB), val_c.reshape(N_DOM, NB, K, TILE, TILE)))
    gathered = summed.reshape(N_DOM * NB * TILE, D).astype(jnp.bfloat16)
    mixed = jnp.dot(hidden, w_one, preferred_element_type=jnp.float32) + jnp.dot(gathered, w_two, preferred_element_type=jnp.float32)
    center = mixed - lax.optimization_barrier(jnp.mean(mixed, axis=1, keepdims=True))
    spread = lax.optimization_barrier(jnp.mean(center * center, axis=1, keepdims=True))
    scaled = center * lax.rsqrt(spread + norm_eps) * gain_one.astype(jnp.float32) + bias_one.astype(jnp.float32)
    return jnp.maximum(scaled, 0.0).astype(jnp.bfloat16)

def reference(features, send_rows, send_len, tile_src, tile_count, tile_val, w_self, w_neigh, gain, bias):
    per_layer = [[] for layer_id in range(LAYERS)]
    for span_id in range(SPANS):
        hidden = features[span_id]
        for layer_id in range(LAYERS):
            hidden = sage_layer(hidden, send_rows[span_id], send_len[span_id], tile_src[span_id], tile_count[span_id], tile_val[span_id], w_self[layer_id], w_neigh[layer_id], gain[layer_id], bias[layer_id])
            per_layer[layer_id].append(hidden)
    return jnp.stack([jnp.stack(layer_acts) for layer_acts in per_layer])
```

```python
import jax
import jax.numpy as jnp
from jax import lax
from jax.experimental import pallas as pl
from jax.experimental.pallas import tpu as pltpu
from jax.sharding import PartitionSpec as P

norm_eps = 1e-05
MESH = pl.DeviceIdType.MESH
F32, BF16, I32 = jnp.float32, jnp.bfloat16, jnp.int32
LAYERS = 4
RING = 4
CHIPS = 16
TILE = 128
ROWS = 512
D = 512
FS = 32
AUX = 128


def kernel(
    feat_hbm, rows_ref, len_ref, src_ref, cnt_ref, tv_hbm, ws_ref, wn_ref, gain_ref, bias_ref,
    out_hbm,
    feat, xt, wp, tv, meta, m1a, px, m1b, m1c, xc, xf, aggs, agg, outr, pre, qs,
    loc_sem, tv_s, tv_r, t1_s, t1_r, fw_s, fw_r, t2_s, t2_r, w_s, w_r, o_s, o_r, m_s, m_r, mb_s, mb_r, pm_s, pm_r,
):
    x = lax.axis_index("segment")
    d = lax.axis_index("dom")
    k = lax.rem(d, 2)
    r = lax.div(d, 2)
    y, z = lax.div(r, RING), lax.rem(r, RING)

    def to(o):
        return lax.rem(y + lax.div(o, RING), RING) * RING + lax.rem(z + lax.rem(o, RING), RING)

    def fro(o):
        return (
            lax.rem(y + RING - lax.div(o, RING), RING) * RING
            + lax.rem(z + RING - lax.rem(o, RING), RING)
        )

    def chip(c):
        return {"dom": c * 2 + k}

    partner = {"dom": r * 2 + (1 - k)}

    def seg(j):
        return {"segment": lax.rem(x + j, LAYERS)}

    def rcopy(src, dst, ssem, rsem, dev):
        return pltpu.make_async_remote_copy(
            src_ref=src, dst_ref=dst, send_sem=ssem, recv_sem=rsem, device_id=dev, device_id_type=MESH
        )

    def each(lo, hi, f):
        def body(i, c):
            f(i)
            return c
        lax.fori_loop(lo, hi, body, 0)

    load_f = pltpu.make_async_copy(feat_hbm.at[x], feat, loc_sem.at[0])
    load_t = pltpu.make_async_copy(tv_hbm.at[x], tv.at[r], loc_sem.at[1])
    load_f.start()
    load_t.start()

    barrier = pltpu.get_barrier_semaphore()
    each(1, CHIPS, lambda o: pl.semaphore_signal(barrier, inc=1, device_id=chip(to(o)), device_id_type=MESH))
    pl.semaphore_signal(barrier, inc=1, device_id=partner, device_id_type=MESH)
    for j in range(1, LAYERS):
        pl.semaphore_signal(barrier, inc=1, device_id=seg(j), device_id_type=MESH)

    load_f.wait()
    for b in range(D // TILE):
        xt[0, b * TILE:(b + 1) * TILE, :] = feat[:, b * TILE:(b + 1) * TILE].astype(F32).T.astype(BF16)
    load_t.wait()
    pl.semaphore_wait(barrier, CHIPS - 1 + 1 + LAYERS - 1)

    counter = [0]

    def at(h, da, db, lo, n):
        yy, zz = (y + db, z + da) if h == 0 else (y + da, z + db)
        c = lax.rem(yy + 2 * RING, RING) * RING + lax.rem(zz + 2 * RING, RING)
        return tv.at[c, pl.ds(2 * h + lo, n)]

    def ring_send(h, first, da, db, s, lo, n):
        along_z = (h == 0) == first
        if along_z:
            dev = chip(y * RING + lax.rem(z + s + RING, RING))
        else:
            dev = chip(lax.rem(y + s + RING, RING) * RING + z)
        i = counter[0]
        counter[0] += 1
        ref = at(h, da, db, lo, n)
        c = rcopy(ref, ref, tv_s.at[i], tv_r.at[i], dev)
        c.start()
        return c, (h, da, db, lo, n, i)

    def ring_wait(entry, first, s):
        h, da, db, lo, n, i = entry[1]
        da, db = (da - s, db) if first else (da, db - s)
        ref = at(h, da, db, lo, n)
        rcopy(ref, ref, tv_s.at[i], tv_r.at[i], partner).wait_recv()

    s1, s1b, s2, s2b = {}, {}, {}, {}

    def second(h, da):
        for s in (1, -1):
            s2[h, da, s] = ring_send(h, False, da, 0, s, 0, 2)

    def second_fwd(h, da):
        for s in (1, -1):
            ring_wait(s2[h, da, s], False, s)
            s2b[h, da, s] = ring_send(h, False, da, -s, s, 0 if s == 1 else 1, 1)

    for h in range(2):
        for s in (1, -1):
            s1[h, s] = ring_send(h, True, 0, 0, s, 0, 2)

    def t1_copy(l, o, c):
        return rcopy(
            xt.at[l, pl.ds(pl.multiple_of(c * FS, FS), FS)], xc.at[l, k, r], t1_s.at[l, o], t1_r.at[l, o], chip(c)
        )

    def t1_in(l, o):
        c = fro(o)
        return rcopy(xc.at[l, k, c], xc.at[l, k, c], t1_s.at[l, o], t1_r.at[l, o], partner)

    def fw_copy(l, o, kk):
        c = fro(o)
        return rcopy(xc.at[l, kk, c], xc.at[l, kk, c], fw_s.at[l, o], fw_r.at[l, o], partner)

    def t1_start(l):
        each(1, CHIPS, lambda o: t1_copy(l, o, to(o)).start())
        xc[l, k, r] = xt[l, pl.ds(pl.multiple_of(r * FS, FS), FS), :]
        fw_copy(l, 0, k).start()

    def t1_finish(l):
        def arrive(o):
            t1_in(l, o).wait_recv()
            fw_copy(l, o, k).start()
            xf[k * CHIPS + fro(o)] = xc[l, k, fro(o)].astype(F32)

        xf[k * CHIPS + r] = xc[l, k, r].astype(F32)
        each(1, CHIPS, arrive)

        def other(o):
            fw_copy(l, o, 1 - k).wait_recv()
            xf[(1 - k) * CHIPS + fro(o)] = xc[l, 1 - k, fro(o)].astype(F32)

        each(0, CHIPS, other)

    t1_start(0)
    for h in range(2):
        second(h, 0)

    lane = lax.broadcasted_iota(I32, (1, TILE), 1)
    for p in range(2 * CHIPS):
        live = lane < len_ref[x, 0, p]
        m1a[p % 2, p // 2:p // 2 + 1, :] = jnp.where(live, rows_ref[x, 0, p:p + 1, :], -1)
    pm = rcopy(m1a.at[1 - k], px, pm_s, pm_r, partner)
    pm.start()

    for b in range(D // TILE):
        cols = slice(b * TILE, (b + 1) * TILE)
        wp[x, cols, 0:D] = ws_ref[0, :, cols].astype(F32).T.astype(BF16)
        wp[x, cols, D:2 * D] = wn_ref[0, :, cols].astype(F32).T.astype(BF16)
        wp[x, cols, 2 * D:2 * D + AUX] = jnp.broadcast_to(gain_ref[:, cols].astype(F32), (AUX, TILE)).T.astype(BF16)
        wp[x, cols, 2 * D + AUX:2 * D + 2 * AUX] = (
            jnp.broadcast_to(bias_ref[:, cols].astype(F32), (AUX, TILE)).T.astype(BF16)
        )

    def w_copy(j):
        return rcopy(wp.at[x], wp.at[x], w_s.at[j], w_r.at[j], seg(j))

    for j in range(1, LAYERS):
        w_copy(j).start()

    pm.wait()
    m1b[...] = jnp.zeros(m1b.shape, I32)
    for c in range(CHIPS):
        m1b[c, pl.ds(k, 1), :] = m1a[k, c:c + 1, :]
        m1b[c, pl.ds(1 - k, 1), :] = px[c:c + 1, :]
    m1c[r] = m1b[r]

    def m1_copy(o):
        c = to(o)
        return rcopy(m1b.at[c], m1c.at[r], m_s.at[o], m_r.at[o], chip(c))

    each(1, CHIPS, lambda o: m1_copy(o).start())

    for h in range(2):
        for s in (1, -1):
            ring_wait(s1[h, s], True, s)
            s1b[h, s] = ring_send(h, True, -s, 0, s, 0 if s == 1 else 1, 1)
    for h in range(2):
        for s in (1, -1):
            second(h, -s)

    def m1_wait(o):
        rcopy(m1b.at[fro(o)], m1c.at[fro(o)], m_s.at[o], m_r.at[o], partner).wait_recv()
    each(1, CHIPS, m1_wait)

    picks = jnp.zeros((1, TILE), I32)
    for t in range(16):
        s = src_ref[x, t // 4, t % 4]
        q = jnp.maximum(s - 4, 0)
        row = m1c[q >> 1, pl.ds(q & 1, 1), :]
        row = jnp.where(s < 4, s * TILE + lane, row)
        row = jnp.where(t % 4 < cnt_ref[x, t // 4], row, -1)
        meta[r, t:t + 1, :] = row
        picks = jnp.where(lane == t, jnp.where(s < 4, k * CHIPS + r, (q & 1) * CHIPS + (q >> 1)), picks)
    meta[r, 16:24, :] = jnp.broadcast_to(picks, (8, TILE))

    def meta_copy(o, c, dev):
        return rcopy(meta.at[c], meta.at[c], mb_s.at[o], mb_r.at[o], dev)

    each(1, CHIPS, lambda o: meta_copy(o, r, chip(to(o))).start())

    for h in range(2):
        second_fwd(h, 0)
    for h in range(2):
        for s in (1, -1):
            ring_wait(s1b[h, s], True, s)
        second(h, 2)

    t1_finish(0)
    each(1, CHIPS, lambda o: meta_copy(o, fro(o), partner).wait_recv())
    move = pltpu.make_async_copy(meta.at[:, 16:24, :], qs, loc_sem.at[2])
    move.start()
    move.wait()

    for da in (1, -1, 2):
        for h in range(2):
            second_fwd(h, da)
    for (h, da, s), e in s2b.items():
        ring_wait(e, False, s)

    def gathered(q, idx):
        low = jnp.broadcast_to(idx & (TILE - 1), (FS, TILE))
        high = idx >> 7
        g = jnp.zeros((FS, TILE), F32)
        for b in range(ROWS // TILE):
            part = jnp.take_along_axis(xf[q, :, b * TILE:(b + 1) * TILE], low, axis=1)
            g = jnp.where(high == b, part, g)
        return g.astype(BF16)

    def t2_copy(l, o):
        c = to(o)
        return rcopy(aggs.at[l, c], agg.at[l, r], t2_s.at[l, o], t2_r.at[l, o], chip(c))

    def aggregate(l, o):
        c = to(o)
        for i in range(4):
            gs = [gathered(qs[c, 0, 4 * i + kk], meta[c, 4 * i + kk:4 * i + kk + 1, :]) for kk in range(4)]
            ts = [tv[c, i, kk] for kk in range(4)]
            a = lax.dot_general(
                jnp.concatenate(gs, axis=1), jnp.concatenate(ts, axis=1), (((1,), (1,)), ((), ())),
                preferred_element_type=F32,
            )
            aggs[l, c, :, i * TILE:(i + 1) * TILE] = a.astype(BF16)

    def out_local(l):
        return pltpu.make_async_copy(outr.at[l], out_hbm.at[0, x], loc_sem.at[3])

    def out_remote(l):
        j = lax.rem(x + LAYERS - l, LAYERS)
        return rcopy(outr.at[l], out_hbm.at[0, x], o_s.at[l], o_r.at[j], {"segment": l})

    def send_out(l):
        for b in range(D // TILE):
            outr[l, :, b * TILE:(b + 1) * TILE] = xt[l + 1, b * TILE:(b + 1) * TILE, :].astype(F32).T.astype(BF16)

        @pl.when(x == l)
        def _():
            out_local(l).start()

        @pl.when(x != l)
        def _():
            out_remote(l).start()

    half = ROWS // 2

    def layer(l):
        @pl.when(l > 0)
        def _():
            t1_start(l)
            send_out(l - 1)

        @pl.when(x != l)
        def _():
            j = lax.rem(x + LAYERS - l, LAYERS)
            rcopy(wp.at[l], wp.at[l], w_s.at[j], w_r.at[j], partner).wait_recv()

        for b in range(2):
            pre[b] = jnp.dot(
                wp[l, :, 0:D], xt[l, :, b * half:(b + 1) * half], preferred_element_type=F32
            )

        @pl.when(l > 0)
        def _():
            t1_finish(l)

        def one(o):
            aggregate(l, o)
            t2_copy(l, o).start()

        each(1, CHIPS, one)
        aggregate(l, 0)
        agg[l, r] = aggs[l, r]

        def got(o):
            c = fro(o)
            rcopy(aggs.at[l, c], agg.at[l, c], t2_s.at[l, o], t2_r.at[l, o], partner).wait_recv()
        each(1, CHIPS, got)
        for b in range(2):
            rhs = agg[l, :, :, b * half:(b + 1) * half].reshape(D, half)
            v = pre[b] + jnp.dot(wp[l, :, D:2 * D], rhs, preferred_element_type=F32)
            pre[b] = v - jnp.mean(v, axis=0, keepdims=True)
            v = pre[b]
            scale = lax.rsqrt(jnp.mean(v * v, axis=0, keepdims=True) + norm_eps)
            for e in range(2):
                cols = slice(e * AUX, (e + 1) * AUX)
                g = wp[l, :, 2 * D:2 * D + AUX].astype(F32)
                h = wp[l, :, 2 * D + AUX:2 * D + 2 * AUX].astype(F32)
                w = pre[b, :, cols] * scale[:, cols] * g + h
                xt[l + 1, :, b * half + e * AUX:b * half + (e + 1) * AUX] = jnp.maximum(w, 0.0).astype(BF16)

    each(0, LAYERS, layer)
    send_out(LAYERS - 1)

    for dct in (s1, s1b, s2, s2b):
        for c, _ in dct.values():
            c.wait_send()
    each(1, CHIPS, lambda o: m1_copy(o).wait_send())
    each(1, CHIPS, lambda o: meta_copy(o, r, chip(to(o))).wait_send())
    for j in range(1, LAYERS):
        w_copy(j).wait_send()

    def sent(l):
        def one(o):
            t1_copy(l, o, to(o)).wait_send()
            t2_copy(l, o).wait_send()
            fw_copy(l, o, k).wait_send()
        each(1, CHIPS, one)
        fw_copy(l, 0, k).wait_send()

        @pl.when(x == l)
        def _():
            out_local(l).wait()

        @pl.when(x != l)
        def _():
            out_remote(l).wait_send()

    each(0, LAYERS, sent)
    for j in range(1, LAYERS):
        c = lax.rem(x + j, LAYERS)
        rcopy(outr.at[0], out_hbm.at[0, c], o_s.at[0], o_r.at[j], partner).wait_recv()


def per_device(features, send_rows, send_len, tile_src, tile_count, tile_val, w_self, w_neigh, gain, bias):
    any_, vmem, smem = (pl.BlockSpec(memory_space=s) for s in (pl.ANY, pltpu.VMEM, pltpu.SMEM))
    dma = pltpu.SemaphoreType.DMA
    return pl.pallas_call(
        kernel,
        out_shape=jax.ShapeDtypeStruct((1, 4, ROWS, D), BF16),
        in_specs=[any_, vmem, smem, smem, smem, any_, vmem, vmem, vmem, vmem],
        out_specs=any_,
        scratch_shapes=[
            pltpu.VMEM((ROWS, D), BF16),
            pltpu.VMEM((LAYERS + 1, D, ROWS), BF16),
            pltpu.VMEM((LAYERS, D, 2 * D + 2 * AUX), BF16),
            pltpu.VMEM((CHIPS, 4, 4, TILE, TILE), BF16),
            pltpu.VMEM((CHIPS, 24, TILE), I32),
            pltpu.VMEM((2, CHIPS, TILE), I32),
            pltpu.VMEM((CHIPS, TILE), I32),
            pltpu.VMEM((CHIPS, 8, TILE), I32),
            pltpu.VMEM((CHIPS, 8, TILE), I32),
            pltpu.VMEM((LAYERS, 2, CHIPS, FS, ROWS), BF16),
            pltpu.VMEM((2 * CHIPS, FS, ROWS), F32),
            pltpu.VMEM((LAYERS, CHIPS, FS, ROWS), BF16),
            pltpu.VMEM((LAYERS, CHIPS, FS, ROWS), BF16),
            pltpu.VMEM((LAYERS, ROWS, D), BF16),
            pltpu.VMEM((2, D, ROWS // 2), F32),
            pltpu.SMEM((CHIPS, 8, TILE), I32),
            dma((4,)),
            dma((48,)), dma((48,)),
            dma((LAYERS, CHIPS)), dma((LAYERS, CHIPS)),
            dma((LAYERS, CHIPS)), dma((LAYERS, CHIPS)),
            dma((LAYERS, CHIPS)), dma((LAYERS, CHIPS)),
            dma((LAYERS,)), dma((LAYERS,)),
            dma((LAYERS,)), dma((LAYERS,)),
            dma((CHIPS,)), dma((CHIPS,)),
            dma((CHIPS,)), dma((CHIPS,)),
            dma, dma,
        ],
        compiler_params=pltpu.CompilerParams(collective_id=0, has_side_effects=True, vmem_limit_bytes=60 << 20),
    )(features, send_rows, send_len, tile_src, tile_count, tile_val, w_self, w_neigh, gain, bias)


def solution(mesh):
    in_specs = (
        P(None, "dom", None),
        P(None, "dom", None, None),
        P(None, "dom", None),
        P(None, "dom", None),
        P(None, "dom"),
        P(None, "dom", None, None, None),
        P("segment", None, None),
        P("segment", None, None),
        P("segment", None),
        P("segment", None),
    )
    out_specs = P("segment", None, "dom", None)
    return jax.shard_map(
        per_device, mesh=mesh, in_specs=in_specs, out_specs=out_specs, check_vma=False
    )
```

```python
import jax
import jax.numpy as jnp
from jax import lax
from jax.experimental import pallas as pl
from jax.experimental.pallas import tpu as pltpu
from jax.sharding import PartitionSpec as P

norm_eps = 1e-05
MESH = pl.DeviceIdType.MESH
F32, BF16, I32 = jnp.float32, jnp.bfloat16, jnp.int32
LAYERS = 4
RING = 4
CHIPS = 16
TILE = 128
ROWS = 512
D = 512
FS = 32
AUX = 128
NH = 2
HR = ROWS // NH
BL = 4 // NH


def kernel(
    feat_hbm, rows_ref, len_ref, src_ref, cnt_ref, tv_hbm, ws_ref, wn_ref, gain_ref, bias_ref,
    out_hbm,
    feat, xt, wp, tv, meta, m1a, px, m1b, m1c, xc, xf, aggs, agg, outr, pre, qs,
    loc_sem, ol_sem, tv_s, tv_r, t1_s, t1_r, fw_s, fw_r, t2_s, t2_r, w_s, w_r, wf_s, wf_r, o_s, o_r, m_s, m_r, mb_s, mb_r, pm_s, pm_r,
):
    x = lax.axis_index("segment")
    d = lax.axis_index("dom")
    k = lax.rem(d, 2)
    r = lax.div(d, 2)
    y, z = lax.div(r, RING), lax.rem(r, RING)

    def to(o):
        return lax.rem(y + lax.div(o, RING), RING) * RING + lax.rem(z + lax.rem(o, RING), RING)

    def fro(o):
        return (
            lax.rem(y + RING - lax.div(o, RING), RING) * RING
            + lax.rem(z + RING - lax.rem(o, RING), RING)
        )

    def chip(c):
        return {"dom": c * 2 + k}

    partner = {"dom": r * 2 + (1 - k)}

    def seg(j):
        return {"segment": lax.rem(x + j, LAYERS)}

    def rcopy(src, dst, ssem, rsem, dev):
        return pltpu.make_async_remote_copy(
            src_ref=src, dst_ref=dst, send_sem=ssem, recv_sem=rsem, device_id=dev, device_id_type=MESH
        )

    def each(lo, hi, f):
        def body(i, c):
            f(i)
            return c
        lax.fori_loop(lo, hi, body, 0)

    load_f = pltpu.make_async_copy(feat_hbm.at[x], feat, loc_sem.at[0])
    load_t = pltpu.make_async_copy(tv_hbm.at[x], tv.at[r], loc_sem.at[1])
    load_f.start()
    load_t.start()

    barrier = pltpu.get_barrier_semaphore()
    each(1, CHIPS, lambda o: pl.semaphore_signal(barrier, inc=1, device_id=chip(to(o)), device_id_type=MESH))
    pl.semaphore_signal(barrier, inc=1, device_id=partner, device_id_type=MESH)
    for j in range(1, LAYERS):
        pl.semaphore_signal(barrier, inc=1, device_id=seg(j), device_id_type=MESH)

    load_f.wait()
    for b in range(D // TILE):
        for h in range(NH):
            part = feat[h * HR:(h + 1) * HR, b * TILE:(b + 1) * TILE]
            xt[0, h, b * TILE:(b + 1) * TILE, :] = part.astype(F32).T.astype(BF16)
    load_t.wait()
    pl.semaphore_wait(barrier, CHIPS - 1 + 1 + LAYERS - 1)

    counter = [0]

    def at(h, da, db, lo, n):
        yy, zz = (y + db, z + da) if h == 0 else (y + da, z + db)
        c = lax.rem(yy + 2 * RING, RING) * RING + lax.rem(zz + 2 * RING, RING)
        return tv.at[c, pl.ds(2 * h + lo, n)]

    def ring_send(h, first, da, db, s, lo, n):
        along_z = (h == 0) == first
        if along_z:
            dev = chip(y * RING + lax.rem(z + s + RING, RING))
        else:
            dev = chip(lax.rem(y + s + RING, RING) * RING + z)
        i = counter[0]
        counter[0] += 1
        ref = at(h, da, db, lo, n)
        c = rcopy(ref, ref, tv_s.at[i], tv_r.at[i], dev)
        c.start()
        return c, (h, da, db, lo, n, i)

    def ring_wait(entry, first, s):
        h, da, db, lo, n, i = entry[1]
        da, db = (da - s, db) if first else (da, db - s)
        ref = at(h, da, db, lo, n)
        rcopy(ref, ref, tv_s.at[i], tv_r.at[i], partner).wait_recv()

    s1, s1b, s2, s2b = {}, {}, {}, {}

    def second(h, da):
        for s in (1, -1):
            s2[h, da, s] = ring_send(h, False, da, 0, s, 0, 2)

    def second_fwd(h, da):
        for s in (1, -1):
            ring_wait(s2[h, da, s], False, s)
            s2b[h, da, s] = ring_send(h, False, da, -s, s, 0 if s == 1 else 1, 1)

    for h in range(2):
        for s in (1, -1):
            s1[h, s] = ring_send(h, True, 0, 0, s, 0, 2)

    def t1_copy(l, h, o, c):
        return rcopy(
            xt.at[l, h, pl.ds(pl.multiple_of(c * FS, FS), FS)], xc.at[l, h, k, r],
            t1_s.at[l, h, o], t1_r.at[l, h, o], chip(c),
        )

    def t1_in(l, h, o):
        ref = xc.at[l, h, k, fro(o)]
        return rcopy(ref, ref, t1_s.at[l, h, o], t1_r.at[l, h, o], partner)

    def row_of(dy):
        return lax.rem(y + RING - dy, RING)

    def fw_copy(l, h, dy, kk):
        ref = xc.at[l, h, kk, pl.ds(row_of(dy) * RING, RING)]
        return rcopy(ref, ref, fw_s.at[l, h, dy], fw_r.at[l, h, dy], partner)

    def t1_start(l, h):
        each(1, CHIPS, lambda o: t1_copy(l, h, o, to(o)).start())
        xc[l, h, k, r] = xt[l, h, pl.ds(pl.multiple_of(r * FS, FS), FS), :]

    def widen(l, h, dy, kk):
        def one(e):
            c = row_of(dy) * RING + e
            xf[kk * CHIPS + c, :, h * HR:(h + 1) * HR] = xc[l, h, kk, c].astype(F32)
        each(0, RING, one)

    def t1_finish(l):
        for h in range(NH):
            def arrive(dy):
                @pl.when(dy > 0)
                def _():
                    t1_in(l, h, dy * RING).wait_recv()
                each(1, RING, lambda dz: t1_in(l, h, dy * RING + dz).wait_recv())
                fw_copy(l, h, dy, k).start()
                widen(l, h, dy, k)
            each(0, RING, arrive)
        for h in range(NH):
            def other(dy):
                fw_copy(l, h, dy, 1 - k).wait_recv()
                widen(l, h, dy, 1 - k)
            each(0, RING, other)

    for h in range(NH):
        t1_start(0, h)
    for h in range(2):
        second(h, 0)

    lane = lax.broadcasted_iota(I32, (1, TILE), 1)
    for p in range(2 * CHIPS):
        live = lane < len_ref[x, 0, p]
        m1a[p % 2, p // 2:p // 2 + 1, :] = jnp.where(live, rows_ref[x, 0, p:p + 1, :], -1)
    pm = rcopy(m1a.at[1 - k], px, pm_s, pm_r, partner)
    pm.start()

    for b in range(D // TILE):
        cols = slice(b * TILE, (b + 1) * TILE)
        wp[x, cols, 0:D] = ws_ref[0, :, cols].astype(F32).T.astype(BF16)
        wp[x, cols, D:2 * D] = wn_ref[0, :, cols].astype(F32).T.astype(BF16)
        wp[x, cols, 2 * D:2 * D + AUX] = jnp.broadcast_to(gain_ref[:, cols].astype(F32), (AUX, TILE)).T.astype(BF16)
        wp[x, cols, 2 * D + AUX:2 * D + 2 * AUX] = (
            jnp.broadcast_to(bias_ref[:, cols].astype(F32), (AUX, TILE)).T.astype(BF16)
        )

    def w_part(l, kk):
        return wp.at[l, pl.ds(pl.multiple_of(kk * (D // 2), D // 2), D // 2)]

    def w_copy(j):
        return rcopy(w_part(x, k), w_part(x, k), w_s.at[j], w_r.at[j], seg(j))

    def w_from(j):
        return lax.rem(x + LAYERS - j, LAYERS)

    def wf_copy(j, kk):
        ref = w_part(w_from(j), kk)
        return rcopy(ref, ref, wf_s.at[j], wf_r.at[j], partner)

    def w_forward(j):
        ref = w_part(w_from(j), k)
        rcopy(ref, ref, w_s.at[j], w_r.at[j], partner).wait_recv()
        wf_copy(j, k).start()

    for j in range(1, LAYERS):
        w_copy(j).start()

    pm.wait()
    m1b[...] = jnp.zeros(m1b.shape, I32)
    for c in range(CHIPS):
        m1b[c, pl.ds(k, 1), :] = m1a[k, c:c + 1, :]
        m1b[c, pl.ds(1 - k, 1), :] = px[c:c + 1, :]
    m1c[r] = m1b[r]

    def m1_copy(o):
        c = to(o)
        return rcopy(m1b.at[c], m1c.at[r], m_s.at[o], m_r.at[o], chip(c))

    each(1, CHIPS, lambda o: m1_copy(o).start())

    def gathered(q, idx):
        low = jnp.broadcast_to(idx & (TILE - 1), (FS, TILE))
        high = idx >> 7
        g = jnp.zeros((FS, TILE), F32)
        for b in range(ROWS // TILE):
            part = jnp.take_along_axis(xf[q, :, b * TILE:(b + 1) * TILE], low, axis=1)
            g = jnp.where(high == b, part, g)
        return g.astype(BF16)

    def t2_copy(l, h, o):
        c = to(o)
        return rcopy(aggs.at[l, h, c], agg.at[l, h, r], t2_s.at[l, h, o], t2_r.at[l, h, o], chip(c))

    def send_back(l, h, o):
        own = isinstance(o, int) and o == 0
        c = to(o)
        for b in range(BL):
            i = h * BL + b
            gs = [gathered(qs[c, 0, 4 * i + kk], meta[c, 4 * i + kk:4 * i + kk + 1, :]) for kk in range(4)]
            ts = [tv[c, i, kk] for kk in range(4)]
            a = lax.dot_general(
                jnp.concatenate(gs, axis=1), jnp.concatenate(ts, axis=1), (((1,), (1,)), ((), ())),
                preferred_element_type=F32,
            )
            dst = agg if own else aggs
            dst[l, h, c, :, b * TILE:(b + 1) * TILE] = a.astype(BF16)
        if not own:
            t2_copy(l, h, o).start()

    def out_rows(l, h):
        return outr.at[l, pl.ds(h * HR, HR)], out_hbm.at[0, x, pl.ds(h * HR, HR)]

    def out_local(l, h):
        src, dst = out_rows(l, h)
        return pltpu.make_async_copy(src, dst, ol_sem.at[h])

    def out_remote(l, h):
        j = lax.rem(x + LAYERS - l, LAYERS)
        src, dst = out_rows(l, h)
        return rcopy(src, dst, o_s.at[l, h], o_r.at[j, h], {"segment": l})

    def send_out(l, h):
        for b in range(D // TILE):
            part = xt[l + 1, h, b * TILE:(b + 1) * TILE, :]
            outr[l, h * HR:(h + 1) * HR, b * TILE:(b + 1) * TILE] = part.astype(F32).T.astype(BF16)

        @pl.when(x == l)
        def _():
            out_local(l, h).start()

        @pl.when(x != l)
        def _():
            out_remote(l, h).start()

    def dense(l, h):
        def got(o):
            ref = agg.at[l, h, fro(o)]
            rcopy(ref, ref, t2_s.at[l, h, o], t2_r.at[l, h, o], partner).wait_recv()
        each(1, CHIPS, got)
        rhs = agg[l, h].reshape(D, HR)
        v = pre[h] + jnp.dot(wp[l, :, D:2 * D], rhs, preferred_element_type=F32)
        pre[h] = v - jnp.mean(v, axis=0, keepdims=True)
        v = pre[h]
        scale = lax.rsqrt(jnp.mean(v * v, axis=0, keepdims=True) + norm_eps)
        g = wp[l, :, 2 * D:2 * D + AUX].astype(F32)
        b = wp[l, :, 2 * D + AUX:2 * D + 2 * AUX].astype(F32)
        for e in range(HR // AUX):
            cols = slice(e * AUX, (e + 1) * AUX)
            w = pre[h, :, cols] * scale[:, cols] * g + b
            xt[l + 1, h, :, cols] = jnp.maximum(w, 0.0).astype(BF16)

    def advance(l, h):
        @pl.when(l < LAYERS - 1)
        def _():
            t1_start(l + 1, h)
        send_out(l, h)

    for h in range(2):
        for s in (1, -1):
            ring_wait(s1[h, s], True, s)
            s1b[h, s] = ring_send(h, True, -s, 0, s, 0 if s == 1 else 1, 1)
    for h in range(2):
        for s in (1, -1):
            second(h, -s)

    def m1_wait(o):
        rcopy(m1b.at[fro(o)], m1c.at[fro(o)], m_s.at[o], m_r.at[o], partner).wait_recv()
    each(1, CHIPS, m1_wait)

    picks = jnp.zeros((1, TILE), I32)
    for t in range(16):
        s = src_ref[x, t // 4, t % 4]
        q = jnp.maximum(s - 4, 0)
        row = m1c[q >> 1, pl.ds(q & 1, 1), :]
        row = jnp.where(s < 4, s * TILE + lane, row)
        row = jnp.where(t % 4 < cnt_ref[x, t // 4], row, -1)
        meta[r, t:t + 1, :] = row
        picks = jnp.where(lane == t, jnp.where(s < 4, k * CHIPS + r, (q & 1) * CHIPS + (q >> 1)), picks)
    meta[r, 16:24, :] = jnp.broadcast_to(picks, (8, TILE))

    def meta_copy(o, c, dev):
        return rcopy(meta.at[c], meta.at[c], mb_s.at[o], mb_r.at[o], dev)

    each(1, CHIPS, lambda o: meta_copy(o, r, chip(to(o))).start())

    for h in range(2):
        second_fwd(h, 0)
    for h in range(2):
        for s in (1, -1):
            ring_wait(s1b[h, s], True, s)
        second(h, 2)

    t1_finish(0)
    each(1, CHIPS, lambda o: meta_copy(o, fro(o), partner).wait_recv())
    move = pltpu.make_async_copy(meta.at[:, 16:24, :], qs, loc_sem.at[2])
    move.start()
    move.wait()

    def arrived(names):
        for name in names:
            ring_wait(s2b[name], False, name[2])

    def first_layer(offsets):
        for dy, dz in offsets:
            o = dy % RING * RING + dz % RING
            for h in range(NH):
                send_back(0, h, o)

    first_layer([(0, 0), (0, 1), (0, -1), (1, 0), (-1, 0)])
    for da in (1, -1):
        for h in range(2):
            second_fwd(h, da)
    arrived([(h, 0, s) for h in range(2) for s in (1, -1)])
    first_layer([(0, 2), (2, 0)])
    first_layer([(1, 1), (-1, -1), (1, -1), (-1, 1)])
    for h in range(2):
        second_fwd(h, 2)
    arrived([(h, da, s) for da in (1, -1) for h in range(2) for s in (1, -1)])
    first_layer([(2, 1), (2, -1), (1, 2), (-1, 2)])
    arrived([(h, 2, s) for h in range(2) for s in (1, -1)])
    first_layer([(2, 2)])
    for j in range(1, LAYERS):
        w_forward(j)

    def own_part(l):
        @pl.when(x != l)
        def _():
            j = lax.rem(x + LAYERS - l, LAYERS)
            wf_copy(j, 1 - k).wait_recv()

        for h in range(NH):
            pre[h] = jnp.dot(wp[l, :, 0:D], xt[l, h], preferred_element_type=F32)

    own_part(0)
    for h in range(NH):
        dense(0, h)
        advance(0, h)

    def layer(l):
        own_part(l)
        t1_finish(l)
        for h in range(NH):
            each(1, CHIPS, lambda o: send_back(l, h, o))
            send_back(l, h, 0)
            if h > 0:
                dense(l, h - 1)
                advance(l, h - 1)
        dense(l, NH - 1)
        advance(l, NH - 1)

    each(1, LAYERS, layer)

    for dct in (s1, s1b, s2, s2b):
        for c, _ in dct.values():
            c.wait_send()
    each(1, CHIPS, lambda o: m1_copy(o).wait_send())
    each(1, CHIPS, lambda o: meta_copy(o, r, chip(to(o))).wait_send())
    for j in range(1, LAYERS):
        w_copy(j).wait_send()
        wf_copy(j, k).wait_send()

    def sent(l):
        for h in range(NH):
            def one(o):
                t1_copy(l, h, o, to(o)).wait_send()
                t2_copy(l, h, o).wait_send()
            each(1, CHIPS, one)
            each(0, RING, lambda dy: fw_copy(l, h, dy, k).wait_send())

            @pl.when(x == l)
            def _():
                out_local(l, h).wait()

            @pl.when(x != l)
            def _():
                out_remote(l, h).wait_send()

    each(0, LAYERS, sent)
    for j in range(1, LAYERS):
        c = lax.rem(x + j, LAYERS)
        for h in range(NH):
            src, _ = out_rows(0, h)
            rcopy(src, out_hbm.at[0, c, pl.ds(h * HR, HR)], o_s.at[0, h], o_r.at[j, h], partner).wait_recv()


def per_device(features, send_rows, send_len, tile_src, tile_count, tile_val, w_self, w_neigh, gain, bias):
    any_, vmem, smem = (pl.BlockSpec(memory_space=s) for s in (pl.ANY, pltpu.VMEM, pltpu.SMEM))
    dma = pltpu.SemaphoreType.DMA
    return pl.pallas_call(
        kernel,
        out_shape=jax.ShapeDtypeStruct((1, 4, ROWS, D), BF16),
        in_specs=[any_, vmem, smem, smem, smem, any_, vmem, vmem, vmem, vmem],
        out_specs=any_,
        scratch_shapes=[
            pltpu.VMEM((ROWS, D), BF16),
            pltpu.VMEM((LAYERS + 1, NH, D, HR), BF16),
            pltpu.VMEM((LAYERS, D, 2 * D + 2 * AUX), BF16),
            pltpu.VMEM((CHIPS, 4, 4, TILE, TILE), BF16),
            pltpu.VMEM((CHIPS, 24, TILE), I32),
            pltpu.VMEM((2, CHIPS, TILE), I32),
            pltpu.VMEM((CHIPS, TILE), I32),
            pltpu.VMEM((CHIPS, 8, TILE), I32),
            pltpu.VMEM((CHIPS, 8, TILE), I32),
            pltpu.VMEM((LAYERS, NH, 2, CHIPS, FS, HR), BF16),
            pltpu.VMEM((2 * CHIPS, FS, ROWS), F32),
            pltpu.VMEM((LAYERS, NH, CHIPS, FS, HR), BF16),
            pltpu.VMEM((LAYERS, NH, CHIPS, FS, HR), BF16),
            pltpu.VMEM((LAYERS, ROWS, D), BF16),
            pltpu.VMEM((NH, D, HR), F32),
            pltpu.SMEM((CHIPS, 8, TILE), I32),
            dma((3,)), dma((NH,)),
            dma((48,)), dma((48,)),
            dma((LAYERS, NH, CHIPS)), dma((LAYERS, NH, CHIPS)),
            dma((LAYERS, NH, RING)), dma((LAYERS, NH, RING)),
            dma((LAYERS, NH, CHIPS)), dma((LAYERS, NH, CHIPS)),
            dma((LAYERS,)), dma((LAYERS,)),
            dma((LAYERS,)), dma((LAYERS,)),
            dma((LAYERS, NH)), dma((LAYERS, NH)),
            dma((CHIPS,)), dma((CHIPS,)),
            dma((CHIPS,)), dma((CHIPS,)),
            dma, dma,
        ],
        compiler_params=pltpu.CompilerParams(collective_id=0, has_side_effects=True, vmem_limit_bytes=60 << 20),
    )(features, send_rows, send_len, tile_src, tile_count, tile_val, w_self, w_neigh, gain, bias)


def solution(mesh):
    in_specs = (
        P(None, "dom", None),
        P(None, "dom", None, None),
        P(None, "dom", None),
        P(None, "dom", None),
        P(None, "dom"),
        P(None, "dom", None, None, None),
        P("segment", None, None),
        P("segment", None, None),
        P("segment", None),
        P("segment", None),
    )
    out_specs = P("segment", None, "dom", None)
    return jax.shard_map(
        per_device, mesh=mesh, in_specs=in_specs, out_specs=out_specs, check_vma=False
    )
```

```python
import jax
import jax.numpy as jnp
from jax import lax
from jax.experimental import pallas as pl
from jax.experimental.pallas import tpu as pltpu
from jax.sharding import PartitionSpec as P

norm_eps = 1e-05
MESH = pl.DeviceIdType.MESH
F32, BF16, I32 = jnp.float32, jnp.bfloat16, jnp.int32
LAYERS = 4
RING = 4
CHIPS = 16
TILE = 128
ROWS = 512
D = 512
FS = 32
AUX = 128
NH = 2
HR = ROWS // NH
BL = 4 // NH


def kernel(
    feat_hbm, rows_ref, len_ref, src_ref, cnt_ref, tv_hbm, ws_ref, wn_ref, gain_ref, bias_ref,
    out_hbm,
    feat, tvs, ga, gb, relay, xt, wp, tv, meta, m1a, px, m1b, m1c, xc, xf, aggs, agg, outr, pre, qs,
    loc_sem, ol_sem, rl_s, rl_r, tv_s, tv_r, t1_s, t1_r, fw_s, fw_r, t2_s, t2_r, w_s, w_r, wf_s, wf_r, o_s, o_r, m_s, m_r, mb_s, mb_r, pm_s, pm_r,
):
    x = lax.axis_index("segment")
    d = lax.axis_index("dom")
    k = lax.rem(d, 2)
    r = lax.div(d, 2)
    y, z = lax.div(r, RING), lax.rem(r, RING)

    def to(o):
        return lax.rem(y + lax.div(o, RING), RING) * RING + lax.rem(z + lax.rem(o, RING), RING)

    def fro(o):
        return (
            lax.rem(y + RING - lax.div(o, RING), RING) * RING
            + lax.rem(z + RING - lax.rem(o, RING), RING)
        )

    def chip(c):
        return {"dom": c * 2 + k}

    partner = {"dom": r * 2 + (1 - k)}

    def seg(j):
        return {"segment": lax.rem(x + j, LAYERS)}

    def rcopy(src, dst, ssem, rsem, dev):
        return pltpu.make_async_remote_copy(
            src_ref=src, dst_ref=dst, send_sem=ssem, recv_sem=rsem, device_id=dev, device_id_type=MESH
        )

    def each(lo, hi, f):
        def body(i, c):
            f(i)
            return c
        lax.fori_loop(lo, hi, body, 0)

    load_f = pltpu.make_async_copy(feat_hbm.at[x], feat, loc_sem.at[0])
    load_t = pltpu.make_async_copy(tv_hbm.at[x], tvs, loc_sem.at[1])
    load_f.start()
    load_t.start()

    barrier = pltpu.get_barrier_semaphore()
    each(1, CHIPS, lambda o: pl.semaphore_signal(barrier, inc=1, device_id=chip(to(o)), device_id_type=MESH))
    pl.semaphore_signal(barrier, inc=1, device_id=partner, device_id_type=MESH)
    for j in range(1, LAYERS):
        pl.semaphore_signal(barrier, inc=1, device_id=seg(j), device_id_type=MESH)

    def transpose_tiles(h):
        for i in range(2 * h, 2 * h + 2):
            for kk in range(4):
                tv[r, i, kk] = tvs[i, kk].astype(F32).T.astype(BF16)

    load_t.wait()
    transpose_tiles(0)
    pl.semaphore_wait(barrier, CHIPS - 1 + 1 + LAYERS - 1)

    counter = [0]

    def at(h, da, db, lo, n):
        yy, zz = (y + db, z + da) if h == 0 else (y + da, z + db)
        c = lax.rem(yy + 2 * RING, RING) * RING + lax.rem(zz + 2 * RING, RING)
        return tv.at[c, pl.ds(2 * h + lo, n)]

    def ring_send(h, first, da, db, s, lo, n):
        along_z = (h == 0) == first
        if along_z:
            dev = chip(y * RING + lax.rem(z + s + RING, RING))
        else:
            dev = chip(lax.rem(y + s + RING, RING) * RING + z)
        i = counter[0]
        counter[0] += 1
        ref = at(h, da, db, lo, n)
        c = rcopy(ref, ref, tv_s.at[i], tv_r.at[i], dev)
        c.start()
        return c, (h, da, db, lo, n, i)

    def ring_wait(entry, first, s):
        h, da, db, lo, n, i = entry[1]
        da, db = (da - s, db) if first else (da, db - s)
        ref = at(h, da, db, lo, n)
        rcopy(ref, ref, tv_s.at[i], tv_r.at[i], partner).wait_recv()

    s1, s1b, s2, s2b = {}, {}, {}, {}

    def second(h, da):
        for s in (1, -1):
            s2[h, da, s] = ring_send(h, False, da, 0, s, 0, 2)

    def second_fwd(h, da):
        for s in (1, -1):
            ring_wait(s2[h, da, s], False, s)
            s2b[h, da, s] = ring_send(h, False, da, -s, s, 0 if s == 1 else 1, 1)

    for h in range(2):
        if h == 1:
            transpose_tiles(1)
        for s in (1, -1):
            s1[h, s] = ring_send(h, True, 0, 0, s, 0, 2)
    load_f.wait()
    for b in range(D // TILE):
        for h in range(NH):
            part = feat[h * HR:(h + 1) * HR, b * TILE:(b + 1) * TILE]
            xt[0, h, b * TILE:(b + 1) * TILE, :] = part.astype(F32).T.astype(BF16)

    def t1_copy(l, h, o, c):
        return rcopy(
            xt.at[l, h, pl.ds(pl.multiple_of(c * FS, FS), FS)], xc.at[l, h, k, r],
            t1_s.at[l, h, o], t1_r.at[l, h, o], chip(c),
        )

    def t1_in(l, h, o):
        ref = xc.at[l, h, k, fro(o)]
        return rcopy(ref, ref, t1_s.at[l, h, o], t1_r.at[l, h, o], partner)

    def row_of(dy):
        return lax.rem(y + RING - dy, RING)

    def fw_copy(l, h, dy, kk):
        ref = xc.at[l, h, kk, pl.ds(row_of(dy) * RING, RING)]
        return rcopy(ref, ref, fw_s.at[l, h, dy], fw_r.at[l, h, dy], partner)

    def t1_start(l, h):
        each(1, CHIPS, lambda o: t1_copy(l, h, o, to(o)).start())
        xc[l, h, k, r] = xt[l, h, pl.ds(pl.multiple_of(r * FS, FS), FS), :]

    def widen(l, h, dy, kk):
        def one(e):
            c = row_of(dy) * RING + e
            xf[kk * CHIPS + c, :, h * HR:(h + 1) * HR] = xc[l, h, kk, c].astype(F32)
        each(0, RING, one)

    def t1_finish(l):
        for h in range(NH):
            def arrive(dy):
                @pl.when(dy > 0)
                def _():
                    t1_in(l, h, dy * RING).wait_recv()
                each(1, RING, lambda dz: t1_in(l, h, dy * RING + dz).wait_recv())
                fw_copy(l, h, dy, k).start()
                widen(l, h, dy, k)
            each(0, RING, arrive)
        for h in range(NH):
            def other(dy):
                fw_copy(l, h, dy, 1 - k).wait_recv()
                widen(l, h, dy, 1 - k)
            each(0, RING, other)

    for h in range(NH):
        t1_start(0, h)
    for h in range(2):
        second(h, 0)

    lane = lax.broadcasted_iota(I32, (1, TILE), 1)
    for p in range(2 * CHIPS):
        live = lane < len_ref[x, 0, p]
        m1a[p % 2, p // 2:p // 2 + 1, :] = jnp.where(live, rows_ref[x, 0, p:p + 1, :], -1)
    pm = rcopy(m1a.at[1 - k], px, pm_s, pm_r, partner)
    pm.start()

    for b in range(D // TILE):
        cols = slice(b * TILE, (b + 1) * TILE)
        wp[x, cols, 0:D] = ws_ref[0, :, cols].astype(F32).T.astype(BF16)
        wp[x, cols, D:2 * D] = wn_ref[0, :, cols].astype(F32).T.astype(BF16)
        wp[x, cols, 2 * D:2 * D + AUX] = jnp.broadcast_to(gain_ref[:, cols].astype(F32), (AUX, TILE)).T.astype(BF16)
        wp[x, cols, 2 * D + AUX:2 * D + 2 * AUX] = (
            jnp.broadcast_to(bias_ref[:, cols].astype(F32), (AUX, TILE)).T.astype(BF16)
        )

    def w_part(l, kk):
        return wp.at[l, pl.ds(pl.multiple_of(kk * (D // 2), D // 2), D // 2)]

    def w_copy(j):
        return rcopy(w_part(x, k), w_part(x, k), w_s.at[j], w_r.at[j], seg(j))

    def w_from(j):
        return lax.rem(x + LAYERS - j, LAYERS)

    def wf_copy(j, kk):
        ref = w_part(w_from(j), kk)
        return rcopy(ref, ref, wf_s.at[j], wf_r.at[j], partner)

    def w_forward(j):
        ref = w_part(w_from(j), k)
        rcopy(ref, ref, w_s.at[j], w_r.at[j], partner).wait_recv()
        wf_copy(j, k).start()

    for j in range(1, LAYERS):
        w_copy(j).start()

    pm.wait()
    m1b[...] = jnp.zeros(m1b.shape, I32)
    for c in range(CHIPS):
        m1b[c, pl.ds(k, 1), :] = m1a[k, c:c + 1, :]
        m1b[c, pl.ds(1 - k, 1), :] = px[c:c + 1, :]
    m1c[r] = m1b[r]

    def m1_copy(o):
        c = to(o)
        return rcopy(m1b.at[c], m1c.at[r], m_s.at[o], m_r.at[o], chip(c))

    each(1, CHIPS, lambda o: m1_copy(o).start())

    def gathered(q, idx):
        low = jnp.broadcast_to(idx & (TILE - 1), (FS, TILE))
        high = idx >> 7
        g = jnp.zeros((FS, TILE), F32)
        for b in range(ROWS // TILE):
            part = jnp.take_along_axis(xf[q, :, b * TILE:(b + 1) * TILE], low, axis=1)
            g = jnp.where(high == b, part, g)
        return g.astype(BF16)

    def t2_copy(l, h, o):
        c = to(o)
        return rcopy(aggs.at[l, h, c], agg.at[l, h, r], t2_s.at[l, h, o], t2_r.at[l, h, o], chip(c))

    def gather(o, blocks, buf):
        c = to(o)
        for b, i in enumerate(blocks):
            for kk in range(4):
                t = 4 * i + kk
                buf[:, (4 * b + kk) * TILE:(4 * b + kk + 1) * TILE] = gathered(qs[c, 0, t], meta[c, t:t + 1, :])

    def multiply(l, o, blocks, buf, dst):
        c = to(o)
        for b, i in enumerate(blocks):
            a = jnp.dot(
                buf[:, 4 * b * TILE:4 * (b + 1) * TILE], tv[c, i].reshape(4 * TILE, TILE), preferred_element_type=F32
            )
            e = i % BL
            dst[l, i // BL, c, :, e * TILE:(e + 1) * TILE] = a.astype(BF16)

    def aggregate(l, h):
        blocks = range(h * BL, (h + 1) * BL)
        gather(1, blocks, ga)

        def two(t):
            o = 2 * t + 1
            multiply(l, o, blocks, ga, aggs)
            gather(o + 1, blocks, gb)
            t2_copy(l, h, o).start()
            multiply(l, o + 1, blocks, gb, aggs)
            gather(o + 2, blocks, ga)
            t2_copy(l, h, o + 1).start()

        each(0, CHIPS // 2 - 1, two)
        multiply(l, CHIPS - 1, blocks, ga, aggs)
        gather(0, blocks, gb)
        t2_copy(l, h, CHIPS - 1).start()
        multiply(l, 0, blocks, gb, agg)

    def out_rows(l, h):
        return outr.at[l, pl.ds(h * HR, HR)], out_hbm.at[0, x, pl.ds(h * HR, HR)]

    def out_local(l, h):
        src, dst = out_rows(l, h)
        return pltpu.make_async_copy(src, dst, ol_sem.at[h])

    def out_remote(l, h):
        j = lax.rem(x + LAYERS - l, LAYERS)
        src, dst = out_rows(l, h)
        return rcopy(src, dst, o_s.at[l, h], o_r.at[j, h], {"segment": l})

    last = LAYERS - 1

    def relay_in(h):
        return rcopy(
            outr.at[last, pl.ds(h * HR, HR)], relay, rl_s.at[h], rl_r, {"segment": last - 1 if h == 0 else 0}
        )

    def relay_out(h):
        return rcopy(relay, out_hbm.at[0, 1, pl.ds(h * HR, HR)], rl_s.at[NH], o_r.at[2, h], {"segment": last})

    def send_out(l, h):
        for b in range(D // TILE):
            part = xt[l + 1, h, b * TILE:(b + 1) * TILE, :]
            outr[l, h * HR:(h + 1) * HR, b * TILE:(b + 1) * TILE] = part.astype(F32).T.astype(BF16)

        @pl.when(x == l)
        def _():
            out_local(l, h).start()

        far = (x == 1) & (l == last)

        @pl.when((x != l) & jnp.logical_not(far))
        def _():
            out_remote(l, h).start()

        @pl.when(far)
        def _():
            relay_in(h).start()

    def dense(l, h):
        def got(o):
            ref = agg.at[l, h, fro(o)]
            rcopy(ref, ref, t2_s.at[l, h, o], t2_r.at[l, h, o], partner).wait_recv()
        each(1, CHIPS, got)
        rhs = agg[l, h].reshape(D, HR)
        v = pre[h] + jnp.dot(wp[l, :, D:2 * D], rhs, preferred_element_type=F32)
        pre[h] = v - jnp.mean(v, axis=0, keepdims=True)
        v = pre[h]
        scale = lax.rsqrt(jnp.mean(v * v, axis=0, keepdims=True) + norm_eps)
        g = wp[l, :, 2 * D:2 * D + AUX].astype(F32)
        b = wp[l, :, 2 * D + AUX:2 * D + 2 * AUX].astype(F32)
        for e in range(HR // AUX):
            cols = slice(e * AUX, (e + 1) * AUX)
            w = pre[h, :, cols] * scale[:, cols] * g + b
            xt[l + 1, h, :, cols] = jnp.maximum(w, 0.0).astype(BF16)

    def advance(l, h):
        @pl.when(l < LAYERS - 1)
        def _():
            t1_start(l + 1, h)
        send_out(l, h)

    for h in range(2):
        for s in (1, -1):
            ring_wait(s1[h, s], True, s)
            s1b[h, s] = ring_send(h, True, -s, 0, s, 0 if s == 1 else 1, 1)
    for h in range(2):
        for s in (1, -1):
            second(h, -s)

    def m1_wait(o):
        rcopy(m1b.at[fro(o)], m1c.at[fro(o)], m_s.at[o], m_r.at[o], partner).wait_recv()
    each(1, CHIPS, m1_wait)

    picks = jnp.zeros((1, TILE), I32)
    for t in range(16):
        s = src_ref[x, t // 4, t % 4]
        q = jnp.maximum(s - 4, 0)
        row = m1c[q >> 1, pl.ds(q & 1, 1), :]
        row = jnp.where(s < 4, s * TILE + lane, row)
        row = jnp.where(t % 4 < cnt_ref[x, t // 4], row, -1)
        meta[r, t:t + 1, :] = row
        picks = jnp.where(lane == t, jnp.where(s < 4, k * CHIPS + r, (q & 1) * CHIPS + (q >> 1)), picks)
    meta[r, 16:24, :] = jnp.broadcast_to(picks, (8, TILE))

    def meta_copy(o, c, dev):
        return rcopy(meta.at[c], meta.at[c], mb_s.at[o], mb_r.at[o], dev)

    each(1, CHIPS, lambda o: meta_copy(o, r, chip(to(o))).start())

    for h in range(2):
        second_fwd(h, 0)
    for h in range(2):
        for s in (1, -1):
            ring_wait(s1b[h, s], True, s)
        second(h, 2)

    t1_finish(0)
    each(1, CHIPS, lambda o: meta_copy(o, fro(o), partner).wait_recv())
    move = pltpu.make_async_copy(meta.at[:, 16:24, :], qs, loc_sem.at[2])
    move.start()
    move.wait()

    def arrived(names):
        for name in names:
            ring_wait(s2b[name], False, name[2])

    order = [
        (0, 0), (0, 1), (0, -1), (1, 0), (-1, 0), (0, 2), (2, 0), (1, 1), (-1, -1), (1, -1), (-1, 1),
        (2, 1), (2, -1), (1, 2), (-1, 2), (2, 2),
    ]
    offsets = [dy % RING * RING + dz % RING for dy, dz in order]
    bufs = (ga, gb)
    gather(offsets[0], range(4), ga)

    def first_layer(lo, hi):
        for u in range(lo, hi):
            o = offsets[u]
            multiply(0, o, range(4), bufs[u % 2], aggs if o else agg)
            if u + 1 < CHIPS:
                gather(offsets[u + 1], range(4), bufs[(u + 1) % 2])
            if o:
                for h in range(NH):
                    t2_copy(0, h, o).start()

    first_layer(0, 5)
    for da in (1, -1):
        for h in range(2):
            second_fwd(h, da)
    arrived([(h, 0, s) for h in range(2) for s in (1, -1)])
    first_layer(5, 11)
    for h in range(2):
        second_fwd(h, 2)
    arrived([(h, da, s) for da in (1, -1) for h in range(2) for s in (1, -1)])
    first_layer(11, 15)
    arrived([(h, 2, s) for h in range(2) for s in (1, -1)])
    first_layer(15, 16)
    for j in range(1, LAYERS):
        w_forward(j)

    def own_part(l):
        @pl.when(x != l)
        def _():
            j = lax.rem(x + LAYERS - l, LAYERS)
            wf_copy(j, 1 - k).wait_recv()

        for h in range(NH):
            pre[h] = jnp.dot(wp[l, :, 0:D], xt[l, h], preferred_element_type=F32)

    own_part(0)
    for h in range(NH):
        dense(0, h)
        advance(0, h)

    def layer(l):
        own_part(l)
        t1_finish(l)
        for h in range(NH):
            aggregate(l, h)
            if h > 0:
                dense(l, h - 1)
                advance(l, h - 1)
        dense(l, NH - 1)
        advance(l, NH - 1)

    each(1, LAYERS, layer)

    for h, at_x in ((0, last - 1), (1, 0)):
        @pl.when(x == at_x)
        def _():
            relay_in(h).wait_recv()
            relay_out(h).start()
            relay_out(h).wait_send()

    for dct in (s1, s1b, s2, s2b):
        for c, _ in dct.values():
            c.wait_send()
    each(1, CHIPS, lambda o: m1_copy(o).wait_send())
    each(1, CHIPS, lambda o: meta_copy(o, r, chip(to(o))).wait_send())
    for j in range(1, LAYERS):
        w_copy(j).wait_send()
        wf_copy(j, k).wait_send()

    def sent(l):
        for h in range(NH):
            def one(o):
                t1_copy(l, h, o, to(o)).wait_send()
                t2_copy(l, h, o).wait_send()
            each(1, CHIPS, one)
            each(0, RING, lambda dy: fw_copy(l, h, dy, k).wait_send())

            @pl.when(x == l)
            def _():
                out_local(l, h).wait()

            far = (x == 1) & (l == last)

            @pl.when((x != l) & jnp.logical_not(far))
            def _():
                out_remote(l, h).wait_send()

            @pl.when(far)
            def _():
                relay_in(h).wait_send()

    each(0, LAYERS, sent)
    for j in range(1, LAYERS):
        c = lax.rem(x + j, LAYERS)
        for h in range(NH):
            src, _ = out_rows(0, h)
            rcopy(src, out_hbm.at[0, c, pl.ds(h * HR, HR)], o_s.at[0, h], o_r.at[j, h], partner).wait_recv()


def per_device(features, send_rows, send_len, tile_src, tile_count, tile_val, w_self, w_neigh, gain, bias):
    any_, vmem, smem = (pl.BlockSpec(memory_space=s) for s in (pl.ANY, pltpu.VMEM, pltpu.SMEM))
    dma = pltpu.SemaphoreType.DMA
    return pl.pallas_call(
        kernel,
        out_shape=jax.ShapeDtypeStruct((1, 4, ROWS, D), BF16),
        in_specs=[any_, vmem, smem, smem, smem, any_, vmem, vmem, vmem, vmem],
        out_specs=any_,
        scratch_shapes=[
            pltpu.VMEM((ROWS, D), BF16),
            pltpu.VMEM((4, 4, TILE, TILE), BF16),
            pltpu.VMEM((FS, 16 * TILE), BF16),
            pltpu.VMEM((FS, 16 * TILE), BF16),
            pltpu.VMEM((HR, D), BF16),
            pltpu.VMEM((LAYERS + 1, NH, D, HR), BF16),
            pltpu.VMEM((LAYERS, D, 2 * D + 2 * AUX), BF16),
            pltpu.VMEM((CHIPS, 4, 4, TILE, TILE), BF16),
            pltpu.VMEM((CHIPS, 24, TILE), I32),
            pltpu.VMEM((2, CHIPS, TILE), I32),
            pltpu.VMEM((CHIPS, TILE), I32),
            pltpu.VMEM((CHIPS, 8, TILE), I32),
            pltpu.VMEM((CHIPS, 8, TILE), I32),
            pltpu.VMEM((LAYERS, NH, 2, CHIPS, FS, HR), BF16),
            pltpu.VMEM((2 * CHIPS, FS, ROWS), F32),
            pltpu.VMEM((LAYERS, NH, CHIPS, FS, HR), BF16),
            pltpu.VMEM((LAYERS, NH, CHIPS, FS, HR), BF16),
            pltpu.VMEM((LAYERS, ROWS, D), BF16),
            pltpu.VMEM((NH, D, HR), F32),
            pltpu.SMEM((CHIPS, 8, TILE), I32),
            dma((3,)), dma((NH,)), dma((NH + 1,)), dma,
            dma((48,)), dma((48,)),
            dma((LAYERS, NH, CHIPS)), dma((LAYERS, NH, CHIPS)),
            dma((LAYERS, NH, RING)), dma((LAYERS, NH, RING)),
            dma((LAYERS, NH, CHIPS)), dma((LAYERS, NH, CHIPS)),
            dma((LAYERS,)), dma((LAYERS,)),
            dma((LAYERS,)), dma((LAYERS,)),
            dma((LAYERS, NH)), dma((LAYERS, NH)),
            dma((CHIPS,)), dma((CHIPS,)),
            dma((CHIPS,)), dma((CHIPS,)),
            dma, dma,
        ],
        compiler_params=pltpu.CompilerParams(collective_id=0, has_side_effects=True, vmem_limit_bytes=60 << 20),
    )(features, send_rows, send_len, tile_src, tile_count, tile_val, w_self, w_neigh, gain, bias)


def solution(mesh):
    in_specs = (
        P(None, "dom", None),
        P(None, "dom", None, None),
        P(None, "dom", None),
        P(None, "dom", None),
        P(None, "dom"),
        P(None, "dom", None, None, None),
        P("segment", None, None),
        P("segment", None, None),
        P("segment", None),
        P("segment", None),
    )
    out_specs = P("segment", None, "dom", None)
    return jax.shard_map(
        per_device, mesh=mesh, in_specs=in_specs, out_specs=out_specs, check_vma=False
    )
```

```python
import jax
import jax.numpy as jnp
from jax import lax
from jax.experimental import pallas as pl
from jax.experimental.pallas import tpu as pltpu
from jax.sharding import PartitionSpec as P

norm_eps = 1e-05
MESH = pl.DeviceIdType.MESH
F32, BF16, I32 = jnp.float32, jnp.bfloat16, jnp.int32
LAYERS = 4
RING = 4
CHIPS = 16
TILE = 128
ROWS = 512
D = 512
FS = 32
AUX = 128
NH = 2
HR = ROWS // NH
BL = 4 // NH
OH = 2
OR = ROWS // OH


def kernel(
    feat_hbm, rows_ref, len_ref, src_ref, cnt_ref, tv_hbm, ws_ref, wn_ref, gain_ref, bias_ref,
    out_hbm,
    feat, tvs, ga, gb, relay, xt, wp, tv, meta, m1a, px, m1b, m1c, xc, xf, aggs, agg, outr, pre, qs,
    loc_sem, ol_sem, rl_s, rl_r, tv_s, tv_r, t1_s, t1_r, fw_s, fw_r, t2_s, t2_r, w_s, w_r, wf_s, wf_r, o_s, o_r, m_s, m_r, mb_s, mb_r, pm_s, pm_r,
):
    x = lax.axis_index("segment")
    d = lax.axis_index("dom")
    k = lax.rem(d, 2)
    r = lax.div(d, 2)
    y, z = lax.div(r, RING), lax.rem(r, RING)

    def to(o):
        return lax.rem(y + lax.div(o, RING), RING) * RING + lax.rem(z + lax.rem(o, RING), RING)

    def fro(o):
        return (
            lax.rem(y + RING - lax.div(o, RING), RING) * RING
            + lax.rem(z + RING - lax.rem(o, RING), RING)
        )

    def chip(c):
        return {"dom": c * 2 + k}

    partner = {"dom": r * 2 + (1 - k)}

    def seg(j):
        return {"segment": lax.rem(x + j, LAYERS)}

    def rcopy(src, dst, ssem, rsem, dev):
        return pltpu.make_async_remote_copy(
            src_ref=src, dst_ref=dst, send_sem=ssem, recv_sem=rsem, device_id=dev, device_id_type=MESH
        )

    def each(lo, hi, f):
        def body(i, c):
            f(i)
            return c
        lax.fori_loop(lo, hi, body, 0)

    load_f = pltpu.make_async_copy(feat_hbm.at[x], feat, loc_sem.at[0])
    load_t = pltpu.make_async_copy(tv_hbm.at[x], tvs, loc_sem.at[1])
    load_f.start()
    load_t.start()

    barrier = pltpu.get_barrier_semaphore()
    each(1, CHIPS, lambda o: pl.semaphore_signal(barrier, inc=1, device_id=chip(to(o)), device_id_type=MESH))
    pl.semaphore_signal(barrier, inc=1, device_id=partner, device_id_type=MESH)
    for j in range(1, LAYERS):
        pl.semaphore_signal(barrier, inc=1, device_id=seg(j), device_id_type=MESH)

    def transpose_tiles(h):
        for i in range(2 * h, 2 * h + 2):
            for kk in range(4):
                tv[r, i, kk] = tvs[i, kk].astype(F32).T.astype(BF16)

    load_t.wait()
    transpose_tiles(0)
    pl.semaphore_wait(barrier, CHIPS - 1 + 1 + LAYERS - 1)

    counter = [0]

    def at(h, da, db, lo, n):
        yy, zz = (y + db, z + da) if h == 0 else (y + da, z + db)
        c = lax.rem(yy + 2 * RING, RING) * RING + lax.rem(zz + 2 * RING, RING)
        return tv.at[c, pl.ds(2 * h + lo, n)]

    def ring_send(h, first, da, db, s, lo, n):
        along_z = (h == 0) == first
        if along_z:
            dev = chip(y * RING + lax.rem(z + s + RING, RING))
        else:
            dev = chip(lax.rem(y + s + RING, RING) * RING + z)
        i = counter[0]
        counter[0] += 1
        ref = at(h, da, db, lo, n)
        c = rcopy(ref, ref, tv_s.at[i], tv_r.at[i], dev)
        c.start()
        return c, (h, da, db, lo, n, i)

    def ring_wait(entry, first, s):
        h, da, db, lo, n, i = entry[1]
        da, db = (da - s, db) if first else (da, db - s)
        ref = at(h, da, db, lo, n)
        rcopy(ref, ref, tv_s.at[i], tv_r.at[i], partner).wait_recv()

    s1, s1b, s2, s2b = {}, {}, {}, {}

    def second(h, da):
        for s in (1, -1):
            s2[h, da, s] = ring_send(h, False, da, 0, s, 0, 2)

    def second_fwd(h, da):
        for s in (1, -1):
            ring_wait(s2[h, da, s], False, s)
            s2b[h, da, s] = ring_send(h, False, da, -s, s, 0 if s == 1 else 1, 1)

    for h in range(2):
        if h == 1:
            transpose_tiles(1)
        for s in (1, -1):
            s1[h, s] = ring_send(h, True, 0, 0, s, 0, 2)
    load_f.wait()
    for b in range(D // TILE):
        for h in range(NH):
            part = feat[h * HR:(h + 1) * HR, b * TILE:(b + 1) * TILE]
            xt[0, h, b * TILE:(b + 1) * TILE, :] = part.astype(F32).T.astype(BF16)

    def t1_copy(l, h, c):
        return rcopy(
            xt.at[l, h, pl.ds(pl.multiple_of(c * FS, FS), FS)], xc.at[l, h, k, r], t1_s.at[l, h], t1_r.at[l, h], chip(c)
        )

    def t1_all(l, h):
        ref = xc.at[l, h, k, pl.ds(0, CHIPS - 1)]
        return rcopy(ref, ref, t1_s.at[l, h], t1_r.at[l, h], partner)

    def fw_copy(l, h, kk):
        ref = xc.at[l, h, kk]
        return rcopy(ref, ref, fw_s.at[l, h], fw_r.at[l, h], partner)

    def t1_start(l, h):
        each(1, CHIPS, lambda o: t1_copy(l, h, to(CHIPS - o)).start())
        xc[l, h, k, r] = xt[l, h, pl.ds(pl.multiple_of(r * FS, FS), FS), :]

    def widen(l, h, kk):
        def four(g):
            for e in range(RING):
                c = g * RING + e
                xf[kk * CHIPS + c, :, h * HR:(h + 1) * HR] = xc[l, h, kk, c].astype(F32)
        each(0, CHIPS // RING, four)

    def t1_finish(l):
        for h in range(NH):
            t1_all(l, h).wait_recv()
            fw_copy(l, h, k).start()
            widen(l, h, k)
        for h in range(NH):
            fw_copy(l, h, 1 - k).wait_recv()
            widen(l, h, 1 - k)

    for h in range(NH):
        t1_start(0, h)
    for h in range(2):
        second(h, 0)

    lane = lax.broadcasted_iota(I32, (1, TILE), 1)
    for p in range(2 * CHIPS):
        live = lane < len_ref[x, 0, p]
        m1a[p % 2, p // 2:p // 2 + 1, :] = jnp.where(live, rows_ref[x, 0, p:p + 1, :], -1)
    pm = rcopy(m1a.at[1 - k], px, pm_s, pm_r, partner)
    pm.start()

    for b in range(D // TILE):
        cols = slice(b * TILE, (b + 1) * TILE)
        wp[x, cols, 0:D] = ws_ref[0, :, cols].astype(F32).T.astype(BF16)
        wp[x, cols, D:2 * D] = wn_ref[0, :, cols].astype(F32).T.astype(BF16)
        wp[x, cols, 2 * D:2 * D + AUX] = jnp.broadcast_to(gain_ref[:, cols].astype(F32), (AUX, TILE)).T.astype(BF16)
        wp[x, cols, 2 * D + AUX:2 * D + 2 * AUX] = (
            jnp.broadcast_to(bias_ref[:, cols].astype(F32), (AUX, TILE)).T.astype(BF16)
        )

    def w_part(l, kk):
        return wp.at[l, pl.ds(pl.multiple_of(kk * (D // 2), D // 2), D // 2)]

    def w_copy(j):
        return rcopy(w_part(x, k), w_part(x, k), w_s.at[j], w_r.at[j], seg(j))

    def w_from(j):
        return lax.rem(x + LAYERS - j, LAYERS)

    def wf_copy(j, kk):
        ref = w_part(w_from(j), kk)
        return rcopy(ref, ref, wf_s.at[j], wf_r.at[j], partner)

    def w_forward(j):
        ref = w_part(w_from(j), k)
        rcopy(ref, ref, w_s.at[j], w_r.at[j], partner).wait_recv()
        wf_copy(j, k).start()

    for j in range(1, LAYERS):
        w_copy(j).start()

    pm.wait()
    m1b[...] = jnp.zeros(m1b.shape, I32)
    for c in range(CHIPS):
        m1b[c, pl.ds(k, 1), :] = m1a[k, c:c + 1, :]
        m1b[c, pl.ds(1 - k, 1), :] = px[c:c + 1, :]
    m1c[r] = m1b[r]

    def m1_copy(o):
        c = to(o)
        return rcopy(m1b.at[c], m1c.at[r], m_s.at[o], m_r.at[o], chip(c))

    each(1, CHIPS, lambda o: m1_copy(o).start())

    def gathered(q, idx):
        low = jnp.broadcast_to(idx & (TILE - 1), (FS, TILE))
        high = idx >> 7
        g = jnp.zeros((FS, TILE), F32)
        for b in range(ROWS // TILE):
            part = jnp.take_along_axis(xf[q, :, b * TILE:(b + 1) * TILE], low, axis=1)
            g = jnp.where(high == b, part, g)
        return g.astype(BF16)

    def t2_copy(l, h, o):
        c = to(o)
        return rcopy(aggs.at[l, h, c], agg.at[l, h, r], t2_s.at[l, h], t2_r.at[l, h], chip(c))

    def t2_all(l, h):
        ref = agg.at[l, h, pl.ds(0, CHIPS - 1)]
        return rcopy(ref, ref, t2_s.at[l, h], t2_r.at[l, h], partner)

    def gather(o, blocks, buf):
        c = to(o)
        for b, i in enumerate(blocks):
            for kk in range(4):
                t = 4 * i + kk
                buf[:, (4 * b + kk) * TILE:(4 * b + kk + 1) * TILE] = gathered(qs[c, 0, t], meta[c, t:t + 1, :])

    def multiply(l, o, blocks, buf, dst):
        c = to(o)
        for b, i in enumerate(blocks):
            a = jnp.dot(
                buf[:, 4 * b * TILE:4 * (b + 1) * TILE], tv[c, i].reshape(4 * TILE, TILE), preferred_element_type=F32
            )
            e = i % BL
            dst[l, i // BL, c, :, e * TILE:(e + 1) * TILE] = a.astype(BF16)

    def aggregate(l, h):
        blocks = range(h * BL, (h + 1) * BL)
        gather(CHIPS - 1, blocks, ga)

        def two(t):
            o = CHIPS - 1 - 2 * t
            multiply(l, o, blocks, ga, aggs)
            gather(o - 1, blocks, gb)
            t2_copy(l, h, o).start()
            multiply(l, o - 1, blocks, gb, aggs)
            gather(o - 2, blocks, ga)
            t2_copy(l, h, o - 1).start()

        each(0, CHIPS // 2 - 1, two)
        multiply(l, 1, blocks, ga, aggs)
        gather(0, blocks, gb)
        t2_copy(l, h, 1).start()
        multiply(l, 0, blocks, gb, agg)

    def out_rows(l, h):
        return outr.at[l, pl.ds(h * OR, OR)], out_hbm.at[0, x, pl.ds(h * OR, OR)]

    def out_local(l, h):
        src, dst = out_rows(l, h)
        return pltpu.make_async_copy(src, dst, ol_sem.at[h])

    def out_remote(l, h):
        j = lax.rem(x + LAYERS - l, LAYERS)
        src, dst = out_rows(l, h)
        return rcopy(src, dst, o_s.at[l, h], o_r.at[j, h], {"segment": l})

    last = LAYERS - 1

    def relay_in(e):
        src, _ = out_rows(last, e)
        return rcopy(src, relay, rl_s.at[e], rl_r, {"segment": last - 1 if e == 0 else 0})

    def relay_out(e):
        return rcopy(relay, out_hbm.at[0, 1, pl.ds(e * OR, OR)], rl_s.at[e], o_r.at[2, e], {"segment": last})

    def by_place(l, local, remote, relayed):
        far = (x == 1) & (l == last)
        pl.when(x == l)(local)
        pl.when((x != l) & jnp.logical_not(far))(remote)
        pl.when(far)(relayed)

    def send_out(l, h):
        for b in range(D // TILE):
            part = xt[l + 1, h, b * TILE:(b + 1) * TILE, :]
            outr[l, h * HR:(h + 1) * HR, b * TILE:(b + 1) * TILE] = part.astype(F32).T.astype(BF16)
        halves = range(h * OH // NH, (h + 1) * OH // NH)

        def local():
            for e in halves:
                out_local(l, e).start()

        def remote():
            for e in halves:
                out_remote(l, e).start()

        def relayed():
            for e in halves:
                relay_in(e).start()

        by_place(l, local, remote, relayed)

    def dense(l, h):
        t2_all(l, h).wait_recv()
        rhs = agg[l, h].reshape(D, HR)
        v = pre[h] + jnp.dot(wp[l, :, D:2 * D], rhs, preferred_element_type=F32)
        pre[h] = v - jnp.mean(v, axis=0, keepdims=True)
        v = pre[h]
        scale = lax.rsqrt(jnp.mean(v * v, axis=0, keepdims=True) + norm_eps)
        g = wp[l, :, 2 * D:2 * D + AUX].astype(F32)
        b = wp[l, :, 2 * D + AUX:2 * D + 2 * AUX].astype(F32)
        for e in range(HR // AUX):
            cols = slice(e * AUX, (e + 1) * AUX)
            w = pre[h, :, cols] * scale[:, cols] * g + b
            xt[l + 1, h, :, cols] = jnp.maximum(w, 0.0).astype(BF16)

    def advance(l, h):
        @pl.when(l < last)
        def _():
            t1_start(l + 1, h)

        @pl.when(l == last)
        def _():
            send_out(l, h)

        if h == NH - 1:
            @pl.when(l < last)
            def _():
                for e in range(NH):
                    send_out(l, e)

    for h in range(2):
        for s in (1, -1):
            ring_wait(s1[h, s], True, s)
            s1b[h, s] = ring_send(h, True, -s, 0, s, 0 if s == 1 else 1, 1)
    for h in range(2):
        for s in (1, -1):
            second(h, -s)

    def m1_wait(o):
        rcopy(m1b.at[fro(o)], m1c.at[fro(o)], m_s.at[o], m_r.at[o], partner).wait_recv()
    each(1, CHIPS, m1_wait)

    picks = jnp.zeros((1, TILE), I32)
    for t in range(16):
        s = src_ref[x, t // 4, t % 4]
        q = jnp.maximum(s - 4, 0)
        row = m1c[q >> 1, pl.ds(q & 1, 1), :]
        row = jnp.where(s < 4, s * TILE + lane, row)
        row = jnp.where(t % 4 < cnt_ref[x, t // 4], row, -1)
        meta[r, t:t + 1, :] = row
        picks = jnp.where(lane == t, jnp.where(s < 4, k * CHIPS + r, (q & 1) * CHIPS + (q >> 1)), picks)
    meta[r, 16:24, :] = jnp.broadcast_to(picks, (8, TILE))

    def meta_copy(o, c, dev):
        return rcopy(meta.at[c], meta.at[c], mb_s.at[o], mb_r.at[o], dev)

    each(1, CHIPS, lambda o: meta_copy(o, r, chip(to(o))).start())

    for h in range(2):
        second_fwd(h, 0)
    for h in range(2):
        for s in (1, -1):
            ring_wait(s1b[h, s], True, s)
        second(h, 2)

    t1_finish(0)
    each(1, CHIPS, lambda o: meta_copy(o, fro(o), partner).wait_recv())
    move = pltpu.make_async_copy(meta.at[:, 16:24, :], qs, loc_sem.at[2])
    move.start()
    move.wait()

    def arrived(names):
        for name in names:
            ring_wait(s2b[name], False, name[2])

    order = [
        (0, 0), (0, 1), (0, -1), (1, 0), (-1, 0), (0, 2), (2, 0), (1, 1), (-1, -1), (1, -1), (-1, 1),
        (2, 1), (2, -1), (1, 2), (-1, 2), (2, 2),
    ]
    offsets = [dy % RING * RING + dz % RING for dy, dz in order]
    bufs = (ga, gb)
    gather(offsets[0], range(4), ga)

    def first_layer(lo, hi):
        for u in range(lo, hi):
            o = offsets[u]
            multiply(0, o, range(4), bufs[u % 2], aggs if o else agg)
            if u + 1 < CHIPS:
                gather(offsets[u + 1], range(4), bufs[(u + 1) % 2])
            if o:
                for h in range(NH):
                    t2_copy(0, h, o).start()

    first_layer(0, 5)
    for da in (1, -1):
        for h in range(2):
            second_fwd(h, da)
    arrived([(h, 0, s) for h in range(2) for s in (1, -1)])
    first_layer(5, 11)
    for h in range(2):
        second_fwd(h, 2)
    arrived([(h, da, s) for da in (1, -1) for h in range(2) for s in (1, -1)])
    first_layer(11, 15)
    arrived([(h, 2, s) for h in range(2) for s in (1, -1)])
    first_layer(15, 16)
    for j in range(1, LAYERS):
        w_forward(j)

    def own_part(l):
        @pl.when(x != l)
        def _():
            j = lax.rem(x + LAYERS - l, LAYERS)
            wf_copy(j, 1 - k).wait_recv()

        for h in range(NH):
            pre[h] = jnp.dot(wp[l, :, 0:D], xt[l, h], preferred_element_type=F32)

    own_part(0)
    for h in range(NH):
        dense(0, h)
        advance(0, h)

    def layer(l):
        own_part(l)
        t1_finish(l)
        for h in range(NH):
            aggregate(l, h)
            if h > 0:
                dense(l, h - 1)
                advance(l, h - 1)
        dense(l, NH - 1)
        advance(l, NH - 1)

    each(1, LAYERS, layer)

    for e, at_x in ((0, last - 1), (1, 0)):
        @pl.when(x == at_x)
        def _():
            relay_in(e).wait_recv()
            relay_out(e).start()
            relay_out(e).wait_send()

    for dct in (s1, s1b, s2, s2b):
        for c, _ in dct.values():
            c.wait_send()
    each(1, CHIPS, lambda o: m1_copy(o).wait_send())
    each(1, CHIPS, lambda o: meta_copy(o, r, chip(to(o))).wait_send())
    for j in range(1, LAYERS):
        w_copy(j).wait_send()
        wf_copy(j, k).wait_send()

    def sent(l):
        for h in range(NH):
            t1_all(l, h).wait_send()
            t2_all(l, h).wait_send()
            fw_copy(l, h, k).wait_send()

        def local():
            for e in range(OH):
                out_local(l, e).wait()

        def remote():
            for e in range(OH):
                out_remote(l, e).wait_send()

        def relayed():
            for e in range(OH):
                relay_in(e).wait_send()

        by_place(l, local, remote, relayed)

    each(0, LAYERS, sent)
    for j in range(1, LAYERS):
        c = lax.rem(x + j, LAYERS)
        for e in range(OH):
            src, _ = out_rows(0, e)
            rcopy(src, out_hbm.at[0, c, pl.ds(e * OR, OR)], o_s.at[0, e], o_r.at[j, e], partner).wait_recv()


def per_device(features, send_rows, send_len, tile_src, tile_count, tile_val, w_self, w_neigh, gain, bias):
    any_, vmem, smem = (pl.BlockSpec(memory_space=s) for s in (pl.ANY, pltpu.VMEM, pltpu.SMEM))
    dma = pltpu.SemaphoreType.DMA
    return pl.pallas_call(
        kernel,
        out_shape=jax.ShapeDtypeStruct((1, 4, ROWS, D), BF16),
        in_specs=[any_, vmem, smem, smem, smem, any_, vmem, vmem, vmem, vmem],
        out_specs=any_,
        scratch_shapes=[
            pltpu.VMEM((ROWS, D), BF16),
            pltpu.VMEM((4, 4, TILE, TILE), BF16),
            pltpu.VMEM((FS, 16 * TILE), BF16),
            pltpu.VMEM((FS, 16 * TILE), BF16),
            pltpu.VMEM((OR, D), BF16),
            pltpu.VMEM((LAYERS + 1, NH, D, HR), BF16),
            pltpu.VMEM((LAYERS, D, 2 * D + 2 * AUX), BF16),
            pltpu.VMEM((CHIPS, 4, 4, TILE, TILE), BF16),
            pltpu.VMEM((CHIPS, 24, TILE), I32),
            pltpu.VMEM((2, CHIPS, TILE), I32),
            pltpu.VMEM((CHIPS, TILE), I32),
            pltpu.VMEM((CHIPS, 8, TILE), I32),
            pltpu.VMEM((CHIPS, 8, TILE), I32),
            pltpu.VMEM((LAYERS, NH, 2, CHIPS, FS, HR), BF16),
            pltpu.VMEM((2 * CHIPS, FS, ROWS), F32),
            pltpu.VMEM((LAYERS, NH, CHIPS, FS, HR), BF16),
            pltpu.VMEM((LAYERS, NH, CHIPS, FS, HR), BF16),
            pltpu.VMEM((LAYERS, ROWS, D), BF16),
            pltpu.VMEM((NH, D, HR), F32),
            pltpu.SMEM((CHIPS, 8, TILE), I32),
            dma((3,)), dma((OH,)), dma((OH,)), dma,
            dma((48,)), dma((48,)),
            dma((LAYERS, NH)), dma((LAYERS, NH)),
            dma((LAYERS, NH)), dma((LAYERS, NH)),
            dma((LAYERS, NH)), dma((LAYERS, NH)),
            dma((LAYERS,)), dma((LAYERS,)),
            dma((LAYERS,)), dma((LAYERS,)),
            dma((LAYERS, OH)), dma((LAYERS, OH)),
            dma((CHIPS,)), dma((CHIPS,)),
            dma((CHIPS,)), dma((CHIPS,)),
            dma, dma,
        ],
        compiler_params=pltpu.CompilerParams(collective_id=0, has_side_effects=True, vmem_limit_bytes=60 << 20),
    )(features, send_rows, send_len, tile_src, tile_count, tile_val, w_self, w_neigh, gain, bias)


def solution(mesh):
    in_specs = (
        P(None, "dom", None),
        P(None, "dom", None, None),
        P(None, "dom", None),
        P(None, "dom", None),
        P(None, "dom"),
        P(None, "dom", None, None, None),
        P("segment", None, None),
        P("segment", None, None),
        P("segment", None),
        P("segment", None),
    )
    out_specs = P("segment", None, "dom", None)
    return jax.shard_map(
        per_device, mesh=mesh, in_specs=in_specs, out_specs=out_specs, check_vma=False
    )
```

```python
import jax
import jax.numpy as jnp
from jax import lax
from jax.experimental import pallas as pl
from jax.experimental.pallas import tpu as pltpu
from jax.sharding import PartitionSpec as P

norm_eps = 1e-05
MESH = pl.DeviceIdType.MESH
F32, BF16, I32 = jnp.float32, jnp.bfloat16, jnp.int32
LAYERS = 4
RING = 4
CHIPS = 16
TILE = 128
ROWS = 512
D = 512
FS = 32
AUX = 128
NH = 2
HR = ROWS // NH
BL = 4 // NH
OH = 2
OR = ROWS // OH


def kernel(
    feat_hbm, rows_ref, len_ref, src_ref, cnt_ref, tv_hbm, ws_ref, wn_ref, gain_ref, bias_ref,
    out_hbm,
    feat, tvs, ga, gb, relay, xt, wp, tv, meta, m1a, px, m1b, m1c, xc, xf, aggs, agg, outr, pre, qs,
    loc_sem, ol_sem, rl_s, rl_r, tv_s, tv_r, t1_s, t1_r, fw_s, fw_r, t2_s, t2_r, w_s, w_r, wf_s, wf_r, o_s, o_r, m_s, m_r, mb_s, mb_r, pm_s, pm_r,
):
    x = lax.axis_index("segment")
    d = lax.axis_index("dom")
    k = lax.rem(d, 2)
    r = lax.div(d, 2)
    y, z = lax.div(r, RING), lax.rem(r, RING)

    def at_offset(dy, dz):
        return lax.rem(y + dy, RING) * RING + lax.rem(z + dz, RING)

    def to(o):
        return lax.rem(y + lax.div(o, RING), RING) * RING + lax.rem(z + lax.rem(o, RING), RING)

    def fro(o):
        return (
            lax.rem(y + RING - lax.div(o, RING), RING) * RING
            + lax.rem(z + RING - lax.rem(o, RING), RING)
        )

    def chip(c):
        return {"dom": c * 2 + k}

    partner = {"dom": r * 2 + (1 - k)}

    def seg(j):
        return {"segment": lax.rem(x + j, LAYERS)}

    def rcopy(src, dst, ssem, rsem, dev):
        return pltpu.make_async_remote_copy(
            src_ref=src, dst_ref=dst, send_sem=ssem, recv_sem=rsem, device_id=dev, device_id_type=MESH
        )

    def each(lo, hi, f):
        def body(i, c):
            f(i)
            return c
        lax.fori_loop(lo, hi, body, 0)

    load_f = pltpu.make_async_copy(feat_hbm.at[x], feat, loc_sem.at[0])
    load_t = pltpu.make_async_copy(tv_hbm.at[x], tvs, loc_sem.at[1])
    load_f.start()
    load_t.start()

    barrier = pltpu.get_barrier_semaphore()
    each(1, CHIPS, lambda o: pl.semaphore_signal(barrier, inc=1, device_id=chip(to(o)), device_id_type=MESH))
    pl.semaphore_signal(barrier, inc=1, device_id=partner, device_id_type=MESH)
    for j in range(1, LAYERS):
        pl.semaphore_signal(barrier, inc=1, device_id=seg(j), device_id_type=MESH)

    def transpose_tiles(h):
        for i in range(2 * h, 2 * h + 2):
            for kk in range(4):
                tv[r, i, kk] = tvs[i, kk].astype(F32).T.astype(BF16)

    load_t.wait()
    transpose_tiles(0)
    pl.semaphore_wait(barrier, CHIPS - 1 + 1 + LAYERS - 1)

    counter = [0]

    def at(h, da, db, lo, n):
        yy, zz = (y + db, z + da) if h == 0 else (y + da, z + db)
        c = lax.rem(yy + 2 * RING, RING) * RING + lax.rem(zz + 2 * RING, RING)
        return tv.at[c, pl.ds(2 * h + lo, n)]

    def ring_send(h, first, da, db, s, lo, n):
        along_z = (h == 0) == first
        if along_z:
            dev = chip(y * RING + lax.rem(z + s + RING, RING))
        else:
            dev = chip(lax.rem(y + s + RING, RING) * RING + z)
        i = counter[0]
        counter[0] += 1
        ref = at(h, da, db, lo, n)
        c = rcopy(ref, ref, tv_s.at[i], tv_r.at[i], dev)
        c.start()
        return c, (h, da, db, lo, n, i)

    def ring_wait(entry, first, s):
        h, da, db, lo, n, i = entry[1]
        da, db = (da - s, db) if first else (da, db - s)
        ref = at(h, da, db, lo, n)
        rcopy(ref, ref, tv_s.at[i], tv_r.at[i], partner).wait_recv()

    s1, s1b, s2, s2b = {}, {}, {}, {}

    def second(h, da):
        for s in (1, -1):
            s2[h, da, s] = ring_send(h, False, da, 0, s, 0, 2)

    def second_fwd(h, da):
        for s in (1, -1):
            ring_wait(s2[h, da, s], False, s)
            s2b[h, da, s] = ring_send(h, False, da, -s, s, 0 if s == 1 else 1, 1)

    for h in range(2):
        if h == 1:
            transpose_tiles(1)
        for s in (1, -1):
            s1[h, s] = ring_send(h, True, 0, 0, s, 0, 2)
    load_f.wait()
    for b in range(D // TILE):
        for h in range(NH):
            part = feat[h * HR:(h + 1) * HR, b * TILE:(b + 1) * TILE]
            xt[0, h, b * TILE:(b + 1) * TILE, :] = part.astype(F32).T.astype(BF16)

    def t1_copy(l, h, c):
        return rcopy(
            xt.at[l, h, pl.ds(pl.multiple_of(c * FS, FS), FS)], xc.at[l, h, k, r], t1_s.at[l, h], t1_r.at[l, h], chip(c)
        )

    def t1_all(l, h):
        ref = xc.at[l, h, k, pl.ds(0, CHIPS - 1)]
        return rcopy(ref, ref, t1_s.at[l, h], t1_r.at[l, h], partner)

    def fw_copy(l, h, kk):
        ref = xc.at[l, h, kk]
        return rcopy(ref, ref, fw_s.at[l, h], fw_r.at[l, h], partner)

    def t1_start(l, h):
        for dy in (2, 3, 1, 0):
            for dz in (2, 3, 1, 0):
                if dy or dz:
                    t1_copy(l, h, at_offset(dy, dz)).start()
        xc[l, h, k, r] = xt[l, h, pl.ds(pl.multiple_of(r * FS, FS), FS), :]

    def widen(l, h, kk):
        def four(g):
            for e in range(RING):
                c = g * RING + e
                xf[kk * CHIPS + c, :, h * HR:(h + 1) * HR] = xc[l, h, kk, c].astype(F32)
        each(0, CHIPS // RING, four)

    def t1_finish(l):
        for h in range(NH):
            t1_all(l, h).wait_recv()
            fw_copy(l, h, k).start()
            widen(l, h, k)
        for h in range(NH):
            fw_copy(l, h, 1 - k).wait_recv()
            widen(l, h, 1 - k)

    for h in range(NH):
        t1_start(0, h)
    for h in range(2):
        second(h, 0)

    lane = lax.broadcasted_iota(I32, (1, TILE), 1)
    for p in range(2 * CHIPS):
        live = lane < len_ref[x, 0, p]
        m1a[p % 2, p // 2:p // 2 + 1, :] = jnp.where(live, rows_ref[x, 0, p:p + 1, :], -1)
    pm = rcopy(m1a.at[1 - k], px, pm_s, pm_r, partner)
    pm.start()

    for b in range(D // TILE):
        cols = slice(b * TILE, (b + 1) * TILE)
        wp[x, cols, 0:D] = ws_ref[0, :, cols].astype(F32).T.astype(BF16)
        wp[x, cols, D:2 * D] = wn_ref[0, :, cols].astype(F32).T.astype(BF16)
        wp[x, cols, 2 * D:2 * D + AUX] = jnp.broadcast_to(gain_ref[:, cols].astype(F32), (AUX, TILE)).T.astype(BF16)
        wp[x, cols, 2 * D + AUX:2 * D + 2 * AUX] = (
            jnp.broadcast_to(bias_ref[:, cols].astype(F32), (AUX, TILE)).T.astype(BF16)
        )

    def w_part(l, kk):
        return wp.at[l, pl.ds(pl.multiple_of(kk * (D // 2), D // 2), D // 2)]

    def w_copy(j):
        return rcopy(w_part(x, k), w_part(x, k), w_s.at[j], w_r.at[j], seg(j))

    def w_from(j):
        return lax.rem(x + LAYERS - j, LAYERS)

    def wf_copy(j, kk):
        ref = w_part(w_from(j), kk)
        return rcopy(ref, ref, wf_s.at[j], wf_r.at[j], partner)

    def w_forward(j):
        ref = w_part(w_from(j), k)
        rcopy(ref, ref, w_s.at[j], w_r.at[j], partner).wait_recv()
        wf_copy(j, k).start()

    for j in range(1, LAYERS):
        w_copy(j).start()

    pm.wait()
    m1b[...] = jnp.zeros(m1b.shape, I32)
    for c in range(CHIPS):
        m1b[c, pl.ds(k, 1), :] = m1a[k, c:c + 1, :]
        m1b[c, pl.ds(1 - k, 1), :] = px[c:c + 1, :]
    m1c[r] = m1b[r]

    def m1_copy(o):
        c = to(o)
        return rcopy(m1b.at[c], m1c.at[r], m_s.at[o], m_r.at[o], chip(c))

    each(1, CHIPS, lambda o: m1_copy(o).start())

    def gathered(q, idx):
        low = jnp.broadcast_to(idx & (TILE - 1), (FS, TILE))
        high = idx >> 7
        g = jnp.zeros((FS, TILE), F32)
        for b in range(ROWS // TILE):
            part = jnp.take_along_axis(xf[q, :, b * TILE:(b + 1) * TILE], low, axis=1)
            g = jnp.where(high == b, part, g)
        return g.astype(BF16)

    def t2_copy(l, h, c):
        return rcopy(aggs.at[l, h, c], agg.at[l, h, r], t2_s.at[l, h], t2_r.at[l, h], chip(c))

    def t2_all(l, h):
        ref = agg.at[l, h, pl.ds(0, CHIPS - 1)]
        return rcopy(ref, ref, t2_s.at[l, h], t2_r.at[l, h], partner)

    def gather(c, blocks, buf):
        for b, i in enumerate(blocks):
            for kk in range(4):
                t = 4 * i + kk
                buf[:, (4 * b + kk) * TILE:(4 * b + kk + 1) * TILE] = gathered(qs[c, 0, t], meta[c, t:t + 1, :])

    def multiply(l, c, blocks, buf, dst):
        for b, i in enumerate(blocks):
            a = jnp.dot(
                buf[:, 4 * b * TILE:4 * (b + 1) * TILE], tv[c, i].reshape(4 * TILE, TILE), preferred_element_type=F32
            )
            e = i % BL
            dst[l, i // BL, c, :, e * TILE:(e + 1) * TILE] = a.astype(BF16)

    def aggregate(l, h):
        blocks = range(h * BL, (h + 1) * BL)
        bufs = (ga, gb)
        gather(at_offset(RING - 1, RING - 1), blocks, ga)

        def row(dy, own):
            for n in range(RING):
                dz = RING - 1 - n
                c = at_offset(dy, dz)
                mine = own and dz == 0
                multiply(l, c, blocks, bufs[n % 2], agg if mine else aggs)
                if dz:
                    gather(at_offset(dy, dz - 1), blocks, bufs[(n + 1) % 2])
                elif not own:
                    gather(at_offset(dy - 1, RING - 1), blocks, ga)
                if not mine:
                    t2_copy(l, h, c).start()

        each(0, RING - 1, lambda t: row(RING - 1 - t, False))
        row(0, True)

    def out_rows(l, h):
        return outr.at[l, pl.ds(h * OR, OR)], out_hbm.at[0, x, pl.ds(h * OR, OR)]

    def out_local(l, h):
        src, dst = out_rows(l, h)
        return pltpu.make_async_copy(src, dst, ol_sem.at[h])

    def out_remote(l, h):
        j = lax.rem(x + LAYERS - l, LAYERS)
        src, dst = out_rows(l, h)
        return rcopy(src, dst, o_s.at[l, h], o_r.at[j, h], {"segment": l})

    last = LAYERS - 1

    def relay_in(e):
        src, _ = out_rows(last, e)
        return rcopy(src, relay, rl_s.at[e], rl_r, {"segment": last - 1 if e == 0 else 0})

    def relay_out(e):
        return rcopy(relay, out_hbm.at[0, 1, pl.ds(e * OR, OR)], rl_s.at[e], o_r.at[2, e], {"segment": last})

    def by_place(l, local, remote, relayed):
        far = (x == 1) & (l == last)
        pl.when(x == l)(local)
        pl.when((x != l) & jnp.logical_not(far))(remote)
        pl.when(far)(relayed)

    def send_out(l, h):
        for b in range(D // TILE):
            part = xt[l + 1, h, b * TILE:(b + 1) * TILE, :]
            outr[l, h * HR:(h + 1) * HR, b * TILE:(b + 1) * TILE] = part.astype(F32).T.astype(BF16)
        halves = range(h * OH // NH, (h + 1) * OH // NH)

        def local():
            for e in halves:
                out_local(l, e).start()

        def remote():
            for e in halves:
                out_remote(l, e).start()

        def relayed():
            for e in halves:
                relay_in(e).start()

        by_place(l, local, remote, relayed)

    def dense(l, h):
        t2_all(l, h).wait_recv()
        rhs = agg[l, h].reshape(D, HR)
        v = pre[h] + jnp.dot(wp[l, :, D:2 * D], rhs, preferred_element_type=F32)
        pre[h] = v - jnp.mean(v, axis=0, keepdims=True)
        v = pre[h]
        scale = lax.rsqrt(jnp.mean(v * v, axis=0, keepdims=True) + norm_eps)
        g = wp[l, :, 2 * D:2 * D + AUX].astype(F32)
        b = wp[l, :, 2 * D + AUX:2 * D + 2 * AUX].astype(F32)
        for e in range(HR // AUX):
            cols = slice(e * AUX, (e + 1) * AUX)
            w = pre[h, :, cols] * scale[:, cols] * g + b
            xt[l + 1, h, :, cols] = jnp.maximum(w, 0.0).astype(BF16)

    def advance(l, h):
        @pl.when(l < last)
        def _():
            t1_start(l + 1, h)

        @pl.when(l == last)
        def _():
            send_out(l, h)

        if h == NH - 1:
            @pl.when(l < last)
            def _():
                for e in range(NH):
                    send_out(l, e)

    for h in range(2):
        for s in (1, -1):
            ring_wait(s1[h, s], True, s)
            s1b[h, s] = ring_send(h, True, -s, 0, s, 0 if s == 1 else 1, 1)
    for h in range(2):
        for s in (1, -1):
            second(h, -s)

    def m1_wait(o):
        rcopy(m1b.at[fro(o)], m1c.at[fro(o)], m_s.at[o], m_r.at[o], partner).wait_recv()
    each(1, CHIPS, m1_wait)

    picks = jnp.zeros((1, TILE), I32)
    for t in range(16):
        s = src_ref[x, t // 4, t % 4]
        q = jnp.maximum(s - 4, 0)
        row = m1c[q >> 1, pl.ds(q & 1, 1), :]
        row = jnp.where(s < 4, s * TILE + lane, row)
        row = jnp.where(t % 4 < cnt_ref[x, t // 4], row, -1)
        meta[r, t:t + 1, :] = row
        picks = jnp.where(lane == t, jnp.where(s < 4, k * CHIPS + r, (q & 1) * CHIPS + (q >> 1)), picks)
    meta[r, 16:24, :] = jnp.broadcast_to(picks, (8, TILE))

    def meta_copy(o, c, dev):
        return rcopy(meta.at[c], meta.at[c], mb_s.at[o], mb_r.at[o], dev)

    each(1, CHIPS, lambda o: meta_copy(o, r, chip(to(o))).start())

    for h in range(2):
        second_fwd(h, 0)
    for h in range(2):
        for s in (1, -1):
            ring_wait(s1b[h, s], True, s)
        second(h, 2)
    for da in (1, -1):
        for h in range(2):
            second_fwd(h, da)

    t1_finish(0)
    each(1, CHIPS, lambda o: meta_copy(o, fro(o), partner).wait_recv())
    move = pltpu.make_async_copy(meta.at[:, 16:24, :], qs, loc_sem.at[2])
    move.start()
    move.wait()

    def arrived(names):
        for name in names:
            ring_wait(s2b[name], False, name[2])

    order = [
        (0, 0), (0, 1), (0, -1), (1, 0), (-1, 0), (0, 2), (2, 0), (1, 1), (-1, -1), (1, -1), (-1, 1),
        (2, 1), (2, -1), (1, 2), (-1, 2), (2, 2),
    ]
    offsets = [(dy % RING, dz % RING) for dy, dz in order]
    bufs = (ga, gb)
    gather(at_offset(*offsets[0]), range(4), ga)

    def first_layer(lo, hi):
        for u in range(lo, hi):
            c = at_offset(*offsets[u])
            multiply(0, c, range(4), bufs[u % 2], aggs if u else agg)
            if u + 1 < CHIPS:
                gather(at_offset(*offsets[u + 1]), range(4), bufs[(u + 1) % 2])
            if u:
                for h in range(NH):
                    t2_copy(0, h, c).start()

    first_layer(0, 5)
    for h in range(2):
        second_fwd(h, 2)
    arrived([(h, 0, s) for h in range(2) for s in (1, -1)])
    first_layer(5, 11)
    for j in range(1, LAYERS):
        w_forward(j)
    arrived([(h, da, s) for da in (1, -1) for h in range(2) for s in (1, -1)])
    first_layer(11, 15)
    arrived([(h, 2, s) for h in range(2) for s in (1, -1)])
    first_layer(15, 16)

    def own_part(l):
        @pl.when(x != l)
        def _():
            j = lax.rem(x + LAYERS - l, LAYERS)
            wf_copy(j, 1 - k).wait_recv()

        for h in range(NH):
            pre[h] = jnp.dot(wp[l, :, 0:D], xt[l, h], preferred_element_type=F32)

    own_part(0)
    for h in range(NH):
        dense(0, h)
        advance(0, h)

    def layer(l):
        own_part(l)
        t1_finish(l)
        for h in range(NH):
            aggregate(l, h)
            if h > 0:
                dense(l, h - 1)
                advance(l, h - 1)
        dense(l, NH - 1)
        advance(l, NH - 1)

    each(1, LAYERS, layer)

    for e, at_x in ((0, last - 1), (1, 0)):
        @pl.when(x == at_x)
        def _():
            relay_in(e).wait_recv()
            relay_out(e).start()
            relay_out(e).wait_send()

    for dct in (s1, s1b, s2, s2b):
        for c, _ in dct.values():
            c.wait_send()
    each(1, CHIPS, lambda o: m1_copy(o).wait_send())
    each(1, CHIPS, lambda o: meta_copy(o, r, chip(to(o))).wait_send())
    for j in range(1, LAYERS):
        w_copy(j).wait_send()
        wf_copy(j, k).wait_send()

    def sent(l):
        for h in range(NH):
            t1_all(l, h).wait_send()
            t2_all(l, h).wait_send()
            fw_copy(l, h, k).wait_send()

        def local():
            for e in range(OH):
                out_local(l, e).wait()

        def remote():
            for e in range(OH):
                out_remote(l, e).wait_send()

        def relayed():
            for e in range(OH):
                relay_in(e).wait_send()

        by_place(l, local, remote, relayed)

    each(0, LAYERS, sent)
    for j in range(1, LAYERS):
        c = lax.rem(x + j, LAYERS)
        for e in range(OH):
            src, _ = out_rows(0, e)
            rcopy(src, out_hbm.at[0, c, pl.ds(e * OR, OR)], o_s.at[0, e], o_r.at[j, e], partner).wait_recv()


def per_device(features, send_rows, send_len, tile_src, tile_count, tile_val, w_self, w_neigh, gain, bias):
    any_, vmem, smem = (pl.BlockSpec(memory_space=s) for s in (pl.ANY, pltpu.VMEM, pltpu.SMEM))
    dma = pltpu.SemaphoreType.DMA
    return pl.pallas_call(
        kernel,
        out_shape=jax.ShapeDtypeStruct((1, 4, ROWS, D), BF16),
        in_specs=[any_, vmem, smem, smem, smem, any_, vmem, vmem, vmem, vmem],
        out_specs=any_,
        scratch_shapes=[
            pltpu.VMEM((ROWS, D), BF16),
            pltpu.VMEM((4, 4, TILE, TILE), BF16),
            pltpu.VMEM((FS, 16 * TILE), BF16),
            pltpu.VMEM((FS, 16 * TILE), BF16),
            pltpu.VMEM((OR, D), BF16),
            pltpu.VMEM((LAYERS + 1, NH, D, HR), BF16),
            pltpu.VMEM((LAYERS, D, 2 * D + 2 * AUX), BF16),
            pltpu.VMEM((CHIPS, 4, 4, TILE, TILE), BF16),
            pltpu.VMEM((CHIPS, 24, TILE), I32),
            pltpu.VMEM((2, CHIPS, TILE), I32),
            pltpu.VMEM((CHIPS, TILE), I32),
            pltpu.VMEM((CHIPS, 8, TILE), I32),
            pltpu.VMEM((CHIPS, 8, TILE), I32),
            pltpu.VMEM((LAYERS, NH, 2, CHIPS, FS, HR), BF16),
            pltpu.VMEM((2 * CHIPS, FS, ROWS), F32),
            pltpu.VMEM((LAYERS, NH, CHIPS, FS, HR), BF16),
            pltpu.VMEM((LAYERS, NH, CHIPS, FS, HR), BF16),
            pltpu.VMEM((LAYERS, ROWS, D), BF16),
            pltpu.VMEM((NH, D, HR), F32),
            pltpu.SMEM((CHIPS, 8, TILE), I32),
            dma((3,)), dma((OH,)), dma((OH,)), dma,
            dma((48,)), dma((48,)),
            dma((LAYERS, NH)), dma((LAYERS, NH)),
            dma((LAYERS, NH)), dma((LAYERS, NH)),
            dma((LAYERS, NH)), dma((LAYERS, NH)),
            dma((LAYERS,)), dma((LAYERS,)),
            dma((LAYERS,)), dma((LAYERS,)),
            dma((LAYERS, OH)), dma((LAYERS, OH)),
            dma((CHIPS,)), dma((CHIPS,)),
            dma((CHIPS,)), dma((CHIPS,)),
            dma, dma,
        ],
        compiler_params=pltpu.CompilerParams(collective_id=0, has_side_effects=True, vmem_limit_bytes=60 << 20),
    )(features, send_rows, send_len, tile_src, tile_count, tile_val, w_self, w_neigh, gain, bias)


def solution(mesh):
    in_specs = (
        P(None, "dom", None),
        P(None, "dom", None, None),
        P(None, "dom", None),
        P(None, "dom", None),
        P(None, "dom"),
        P(None, "dom", None, None, None),
        P("segment", None, None),
        P("segment", None, None),
        P("segment", None),
        P("segment", None),
    )
    out_specs = P("segment", None, "dom", None)
    return jax.shard_map(
        per_device, mesh=mesh, in_specs=in_specs, out_specs=out_specs, check_vma=False
    )
```

```python
import jax
import jax.numpy as jnp
from jax import lax
from jax.experimental import pallas as pl
from jax.experimental.pallas import tpu as pltpu
from jax.sharding import PartitionSpec as P

norm_eps = 1e-05
MESH = pl.DeviceIdType.MESH
F32, BF16, I32 = jnp.float32, jnp.bfloat16, jnp.int32
LAYERS = 4
RING = 4
CHIPS = 16
TILE = 128
ROWS = 512
D = 512
FS = 32
AUX = 128
NH = 2
HR = ROWS // NH
BL = 4 // NH
OH = 2
OR = ROWS // OH


def kernel(
    feat_hbm, rows_ref, len_ref, src_ref, cnt_ref, tv_hbm, ws_hbm, wn_hbm, gain_ref, bias_ref,
    out_hbm,
    feat, tvs, w_in, ga, gb, relay, xt, wp, tv, meta, m1a, px, m1b, m1c, xc, xf, aggs, agg, outr, pre, qs,
    loc_sem, ol_sem, rl_s, rl_r, ro_s, tv_s, tv_r, t1_s, t1_r, fw_s, fw_r, t2_s, t2_r, w_s, w_r, wf_s, wf_r, o_s, o_r, m_s, m_r, mb_s, mb_r, pm_s, pm_r,
):
    x = lax.axis_index("segment")
    d = lax.axis_index("dom")
    k = lax.rem(d, 2)
    r = lax.div(d, 2)
    y, z = lax.div(r, RING), lax.rem(r, RING)

    def at_offset(dy, dz):
        return lax.rem(y + dy, RING) * RING + lax.rem(z + dz, RING)

    def to(o):
        return lax.rem(y + lax.div(o, RING), RING) * RING + lax.rem(z + lax.rem(o, RING), RING)

    def fro(o):
        return (
            lax.rem(y + RING - lax.div(o, RING), RING) * RING
            + lax.rem(z + RING - lax.rem(o, RING), RING)
        )

    def chip(c):
        return {"dom": c * 2 + k}

    partner = {"dom": r * 2 + (1 - k)}

    def seg(j):
        return {"segment": lax.rem(x + j, LAYERS)}

    def rcopy(src, dst, ssem, rsem, dev):
        return pltpu.make_async_remote_copy(
            src_ref=src, dst_ref=dst, send_sem=ssem, recv_sem=rsem, device_id=dev, device_id_type=MESH
        )

    def each(lo, hi, f):
        def body(i, c):
            f(i)
            return c
        lax.fori_loop(lo, hi, body, 0)

    load_f = pltpu.make_async_copy(feat_hbm.at[x], feat, loc_sem.at[0])
    load_t = pltpu.make_async_copy(tv_hbm.at[x], tvs, loc_sem.at[1])
    load_w = [pltpu.make_async_copy(src.at[0], w_in.at[e], loc_sem.at[3 + e]) for e, src in enumerate((ws_hbm, wn_hbm))]
    load_t.start()
    load_f.start()
    for copy in load_w:
        copy.start()

    barrier = pltpu.get_barrier_semaphore()
    each(1, CHIPS, lambda o: pl.semaphore_signal(barrier, inc=1, device_id=chip(to(o)), device_id_type=MESH))
    pl.semaphore_signal(barrier, inc=1, device_id=partner, device_id_type=MESH)
    for j in range(1, LAYERS):
        pl.semaphore_signal(barrier, inc=1, device_id=seg(j), device_id_type=MESH)

    def transpose_tiles(h):
        for i in range(2 * h, 2 * h + 2):
            for kk in range(4):
                tv[r, i, kk] = tvs[i, kk].astype(F32).T.astype(BF16)

    load_t.wait()
    transpose_tiles(0)
    pl.semaphore_wait(barrier, CHIPS - 1 + 1 + LAYERS - 1)

    counter = [0]

    def at(h, da, db, lo, n):
        yy, zz = (y + db, z + da) if h == 0 else (y + da, z + db)
        c = lax.rem(yy + 2 * RING, RING) * RING + lax.rem(zz + 2 * RING, RING)
        return tv.at[c, pl.ds(2 * h + lo, n)]

    def ring_send(h, first, da, db, s, lo, n):
        along_z = (h == 0) == first
        if along_z:
            dev = chip(y * RING + lax.rem(z + s + RING, RING))
        else:
            dev = chip(lax.rem(y + s + RING, RING) * RING + z)
        i = counter[0]
        counter[0] += 1
        ref = at(h, da, db, lo, n)
        c = rcopy(ref, ref, tv_s.at[i], tv_r.at[i], dev)
        c.start()
        return c, (h, da, db, lo, n, i)

    def ring_wait(entry, first, s):
        h, da, db, lo, n, i = entry[1]
        da, db = (da - s, db) if first else (da, db - s)
        ref = at(h, da, db, lo, n)
        rcopy(ref, ref, tv_s.at[i], tv_r.at[i], partner).wait_recv()

    s1, s1b, s2, s2b = {}, {}, {}, {}

    def second(h, da):
        for s in (1, -1):
            s2[h, da, s] = ring_send(h, False, da, 0, s, 0, 2)

    def second_fwd(h, da):
        for s in (1, -1):
            ring_wait(s2[h, da, s], False, s)
            s2b[h, da, s] = ring_send(h, False, da, -s, s, 0 if s == 1 else 1, 1)

    for h in range(2):
        if h == 1:
            transpose_tiles(1)
        for s in (1, -1):
            s1[h, s] = ring_send(h, True, 0, 0, s, 0, 2)
    load_f.wait()
    for b in range(D // TILE):
        for h in range(NH):
            part = feat[h * HR:(h + 1) * HR, b * TILE:(b + 1) * TILE]
            xt[0, h, b * TILE:(b + 1) * TILE, :] = part.astype(F32).T.astype(BF16)

    def t1_copy(l, h, c):
        return rcopy(
            xt.at[l, h, pl.ds(pl.multiple_of(c * FS, FS), FS)], xc.at[l, h, k, r], t1_s.at[l, h], t1_r.at[l, h], chip(c)
        )

    def t1_all(l, h):
        ref = xc.at[l, h, k, pl.ds(0, CHIPS - 1)]
        return rcopy(ref, ref, t1_s.at[l, h], t1_r.at[l, h], partner)

    def fw_copy(l, h, kk):
        ref = xc.at[l, h, kk]
        return rcopy(ref, ref, fw_s.at[l, h], fw_r.at[l, h], partner)

    def t1_start(l, h):
        for dy in (2, 3, 1, 0):
            for dz in (2, 3, 1, 0):
                if dy or dz:
                    t1_copy(l, h, at_offset(dy, dz)).start()
        xc[l, h, k, r] = xt[l, h, pl.ds(pl.multiple_of(r * FS, FS), FS), :]

    def widen(l, h, kk):
        def four(g):
            for e in range(RING):
                c = g * RING + e
                xf[kk * CHIPS + c, :, h * HR:(h + 1) * HR] = xc[l, h, kk, c].astype(F32)
        each(0, CHIPS // RING, four)

    def t1_finish(l):
        for h in range(NH):
            t1_all(l, h).wait_recv()
            fw_copy(l, h, k).start()
            widen(l, h, k)
        for h in range(NH):
            fw_copy(l, h, 1 - k).wait_recv()
            widen(l, h, 1 - k)

    for h in range(NH):
        t1_start(0, h)
    for h in range(2):
        second(h, 0)

    lane = lax.broadcasted_iota(I32, (1, TILE), 1)
    for p in range(2 * CHIPS):
        live = lane < len_ref[x, 0, p]
        m1a[p % 2, p // 2:p // 2 + 1, :] = jnp.where(live, rows_ref[x, 0, p:p + 1, :], -1)
    pm = rcopy(m1a.at[1 - k], px, pm_s, pm_r, partner)
    pm.start()

    for copy in load_w:
        copy.wait()
    for b in range(D // TILE):
        cols = slice(b * TILE, (b + 1) * TILE)
        wp[x, cols, 0:D] = w_in[0, :, cols].astype(F32).T.astype(BF16)
        wp[x, cols, D:2 * D] = w_in[1, :, cols].astype(F32).T.astype(BF16)
        wp[x, cols, 2 * D:2 * D + AUX] = jnp.broadcast_to(gain_ref[:, cols].astype(F32), (AUX, TILE)).T.astype(BF16)
        wp[x, cols, 2 * D + AUX:2 * D + 2 * AUX] = (
            jnp.broadcast_to(bias_ref[:, cols].astype(F32), (AUX, TILE)).T.astype(BF16)
        )

    def w_part(l, kk):
        return wp.at[l, pl.ds(pl.multiple_of(kk * (D // 2), D // 2), D // 2)]

    def w_copy(j):
        return rcopy(w_part(x, k), w_part(x, k), w_s.at[j], w_r.at[j], seg(j))

    def w_from(j):
        return lax.rem(x + LAYERS - j, LAYERS)

    def wf_copy(j, kk):
        ref = w_part(w_from(j), kk)
        return rcopy(ref, ref, wf_s.at[j], wf_r.at[j], partner)

    def w_forward(j):
        ref = w_part(w_from(j), k)
        rcopy(ref, ref, w_s.at[j], w_r.at[j], partner).wait_recv()
        wf_copy(j, k).start()

    for j in range(1, LAYERS):
        w_copy(j).start()

    pm.wait()
    m1b[...] = jnp.zeros(m1b.shape, I32)
    for c in range(CHIPS):
        m1b[c, pl.ds(k, 1), :] = m1a[k, c:c + 1, :]
        m1b[c, pl.ds(1 - k, 1), :] = px[c:c + 1, :]
    m1c[r] = m1b[r]

    def m1_copy(o):
        c = to(o)
        return rcopy(m1b.at[c], m1c.at[r], m_s.at[o], m_r.at[o], chip(c))

    each(1, CHIPS, lambda o: m1_copy(o).start())

    def gathered(q, idx):
        low = jnp.broadcast_to(idx & (TILE - 1), (FS, TILE))
        high = idx >> 7
        g = jnp.zeros((FS, TILE), F32)
        for b in range(ROWS // TILE):
            part = jnp.take_along_axis(xf[q, :, b * TILE:(b + 1) * TILE], low, axis=1)
            g = jnp.where(high == b, part, g)
        return g.astype(BF16)

    def t2_copy(l, h, c):
        return rcopy(aggs.at[l, h, c], agg.at[l, h, r], t2_s.at[l, h], t2_r.at[l, h], chip(c))

    def t2_all(l, h):
        ref = agg.at[l, h, pl.ds(0, CHIPS - 1)]
        return rcopy(ref, ref, t2_s.at[l, h], t2_r.at[l, h], partner)

    def gather(c, blocks, buf):
        for b, i in enumerate(blocks):
            for kk in range(4):
                t = 4 * i + kk
                buf[:, (4 * b + kk) * TILE:(4 * b + kk + 1) * TILE] = gathered(qs[c, 0, t], meta[c, t:t + 1, :])

    def multiply(l, c, blocks, buf, dst):
        for b, i in enumerate(blocks):
            a = jnp.dot(
                buf[:, 4 * b * TILE:4 * (b + 1) * TILE], tv[c, i].reshape(4 * TILE, TILE), preferred_element_type=F32
            )
            e = i % BL
            dst[l, i // BL, c, :, e * TILE:(e + 1) * TILE] = a.astype(BF16)

    def aggregate(l, h):
        blocks = range(h * BL, (h + 1) * BL)
        bufs = (ga, gb)
        gather(at_offset(RING - 1, RING - 1), blocks, ga)

        def row(dy, own):
            for n in range(RING):
                dz = RING - 1 - n
                c = at_offset(dy, dz)
                mine = own and dz == 0
                multiply(l, c, blocks, bufs[n % 2], agg if mine else aggs)
                if dz:
                    gather(at_offset(dy, dz - 1), blocks, bufs[(n + 1) % 2])
                elif not own:
                    gather(at_offset(dy - 1, RING - 1), blocks, ga)
                if not mine:
                    t2_copy(l, h, c).start()

        each(0, RING - 1, lambda t: row(RING - 1 - t, False))
        row(0, True)

    def out_rows(l, h):
        return outr.at[l, pl.ds(h * OR, OR)], out_hbm.at[0, x, pl.ds(h * OR, OR)]

    def out_local(l, h):
        src, dst = out_rows(l, h)
        return pltpu.make_async_copy(src, dst, ol_sem.at[h])

    def out_remote(l, h):
        j = lax.rem(x + LAYERS - l, LAYERS)
        src, dst = out_rows(l, h)
        return rcopy(src, dst, o_s.at[l, h], o_r.at[j, h], {"segment": l})

    last = LAYERS - 1

    def relay_in(l, e):
        src, _ = out_rows(l, e)
        via = lax.rem(l + (LAYERS - 1 if e == 0 else 1), LAYERS)
        return rcopy(src, relay, rl_s.at[e], rl_r, {"segment": via})

    def relay_out(l, e):
        return rcopy(relay, out_hbm.at[0, l - 2, pl.ds(e * OR, OR)], ro_s, o_r.at[2, e], {"segment": l})

    def pass_on(l, finish):
        for e, at_x in ((0, (l + 3) % LAYERS), (1, (l + 1) % LAYERS)):
            @pl.when(x == at_x)
            def _():
                if finish:
                    relay_out(l, e).wait_send()
                else:
                    relay_in(l, e).wait_recv()
                    relay_out(l, e).start()

    def by_place(l, local, remote, relayed):
        far = x == l - 2
        pl.when(x == l)(local)
        pl.when((x != l) & jnp.logical_not(far))(remote)
        pl.when(far)(relayed)

    def send_out(l, h):
        for b in range(D // TILE):
            part = xt[l + 1, h, b * TILE:(b + 1) * TILE, :]
            outr[l, h * HR:(h + 1) * HR, b * TILE:(b + 1) * TILE] = part.astype(F32).T.astype(BF16)
        halves = range(h * OH // NH, (h + 1) * OH // NH)

        def local():
            for e in halves:
                out_local(l, e).start()

        def remote():
            for e in halves:
                out_remote(l, e).start()

        def relayed():
            for e in halves:
                relay_in(l, e).start()

        by_place(l, local, remote, relayed)

    def dense(l, h):
        t2_all(l, h).wait_recv()
        rhs = agg[l, h].reshape(D, HR)
        v = pre[h] + jnp.dot(wp[l, :, D:2 * D], rhs, preferred_element_type=F32)
        pre[h] = v - jnp.mean(v, axis=0, keepdims=True)
        v = pre[h]
        scale = lax.rsqrt(jnp.mean(v * v, axis=0, keepdims=True) + norm_eps)
        g = wp[l, :, 2 * D:2 * D + AUX].astype(F32)
        b = wp[l, :, 2 * D + AUX:2 * D + 2 * AUX].astype(F32)
        for e in range(HR // AUX):
            cols = slice(e * AUX, (e + 1) * AUX)
            w = pre[h, :, cols] * scale[:, cols] * g + b
            xt[l + 1, h, :, cols] = jnp.maximum(w, 0.0).astype(BF16)

    def advance(l, h):
        @pl.when(l < last)
        def _():
            t1_start(l + 1, h)

        @pl.when(l == last)
        def _():
            send_out(l, h)

        if h == NH - 1:
            @pl.when(l < last)
            def _():
                for e in range(NH):
                    send_out(l, e)

    for h in range(2):
        for s in (1, -1):
            ring_wait(s1[h, s], True, s)
            s1b[h, s] = ring_send(h, True, -s, 0, s, 0 if s == 1 else 1, 1)
    for h in range(2):
        for s in (1, -1):
            second(h, -s)

    def m1_wait(o):
        rcopy(m1b.at[fro(o)], m1c.at[fro(o)], m_s.at[o], m_r.at[o], partner).wait_recv()
    each(1, CHIPS, m1_wait)

    picks = jnp.zeros((1, TILE), I32)
    for t in range(16):
        s = src_ref[x, t // 4, t % 4]
        q = jnp.maximum(s - 4, 0)
        row = m1c[q >> 1, pl.ds(q & 1, 1), :]
        row = jnp.where(s < 4, s * TILE + lane, row)
        row = jnp.where(t % 4 < cnt_ref[x, t // 4], row, -1)
        meta[r, t:t + 1, :] = row
        picks = jnp.where(lane == t, jnp.where(s < 4, k * CHIPS + r, (q & 1) * CHIPS + (q >> 1)), picks)
    meta[r, 16:24, :] = jnp.broadcast_to(picks, (8, TILE))

    def meta_copy(o, c, dev):
        return rcopy(meta.at[c], meta.at[c], mb_s.at[o], mb_r.at[o], dev)

    each(1, CHIPS, lambda o: meta_copy(o, r, chip(to(o))).start())

    for h in range(2):
        second_fwd(h, 0)
    for h in range(2):
        for s in (1, -1):
            ring_wait(s1b[h, s], True, s)
        second(h, 2)
    for da in (1, -1):
        for h in range(2):
            second_fwd(h, da)

    t1_finish(0)
    each(1, CHIPS, lambda o: meta_copy(o, fro(o), partner).wait_recv())
    move = pltpu.make_async_copy(meta.at[:, 16:24, :], qs, loc_sem.at[2])
    move.start()
    move.wait()

    def arrived(names):
        for name in names:
            ring_wait(s2b[name], False, name[2])

    order = [
        (0, 0), (0, 1), (0, -1), (1, 0), (-1, 0), (0, 2), (2, 0), (1, 1), (-1, -1), (1, -1), (-1, 1),
        (2, 1), (2, -1), (1, 2), (-1, 2), (2, 2),
    ]
    offsets = [(dy % RING, dz % RING) for dy, dz in order]
    bufs = (ga, gb)
    gather(at_offset(*offsets[0]), range(4), ga)

    def first_layer(lo, hi):
        for u in range(lo, hi):
            c = at_offset(*offsets[u])
            multiply(0, c, range(4), bufs[u % 2], aggs if u else agg)
            if u + 1 < CHIPS:
                gather(at_offset(*offsets[u + 1]), range(4), bufs[(u + 1) % 2])
            if u:
                for h in range(NH):
                    t2_copy(0, h, c).start()

    first_layer(0, 5)
    for h in range(2):
        second_fwd(h, 2)
    arrived([(h, 0, s) for h in range(2) for s in (1, -1)])
    first_layer(5, 11)
    for j in range(1, LAYERS):
        w_forward(j)
    arrived([(h, da, s) for da in (1, -1) for h in range(2) for s in (1, -1)])
    first_layer(11, 15)
    arrived([(h, 2, s) for h in range(2) for s in (1, -1)])
    first_layer(15, 16)

    def own_part(l):
        @pl.when(x != l)
        def _():
            j = lax.rem(x + LAYERS - l, LAYERS)
            wf_copy(j, 1 - k).wait_recv()

        for h in range(NH):
            pre[h] = jnp.dot(wp[l, :, 0:D], xt[l, h], preferred_element_type=F32)

    own_part(0)
    for h in range(NH):
        dense(0, h)
        advance(0, h)

    def layer(l):
        own_part(l)
        t1_finish(l)
        pl.when(l == last)(lambda: pass_on(last - 1, False))
        for h in range(NH):
            aggregate(l, h)
            if h > 0:
                dense(l, h - 1)
                advance(l, h - 1)
        dense(l, NH - 1)
        advance(l, NH - 1)

    each(1, LAYERS, layer)

    pass_on(last, False)

    for dct in (s1, s1b, s2, s2b):
        for c, _ in dct.values():
            c.wait_send()
    each(1, CHIPS, lambda o: m1_copy(o).wait_send())
    each(1, CHIPS, lambda o: meta_copy(o, r, chip(to(o))).wait_send())
    for j in range(1, LAYERS):
        w_copy(j).wait_send()
        wf_copy(j, k).wait_send()

    def sent(l):
        for h in range(NH):
            t1_all(l, h).wait_send()
            t2_all(l, h).wait_send()
            fw_copy(l, h, k).wait_send()

        def local():
            for e in range(OH):
                out_local(l, e).wait()

        def remote():
            for e in range(OH):
                out_remote(l, e).wait_send()

        def relayed():
            for e in range(OH):
                relay_in(l, e).wait_send()

        by_place(l, local, remote, relayed)

    each(0, LAYERS, sent)
    pass_on(last - 1, True)
    pass_on(last, True)
    for j in range(1, LAYERS):
        c = lax.rem(x + j, LAYERS)
        for e in range(OH):
            src, _ = out_rows(0, e)
            rcopy(src, out_hbm.at[0, c, pl.ds(e * OR, OR)], o_s.at[0, e], o_r.at[j, e], partner).wait_recv()


def per_device(features, send_rows, send_len, tile_src, tile_count, tile_val, w_self, w_neigh, gain, bias):
    any_, vmem, smem = (pl.BlockSpec(memory_space=s) for s in (pl.ANY, pltpu.VMEM, pltpu.SMEM))
    dma = pltpu.SemaphoreType.DMA
    return pl.pallas_call(
        kernel,
        out_shape=jax.ShapeDtypeStruct((1, 4, ROWS, D), BF16),
        in_specs=[any_, vmem, smem, smem, smem, any_, any_, any_, vmem, vmem],
        out_specs=any_,
        scratch_shapes=[
            pltpu.VMEM((ROWS, D), BF16),
            pltpu.VMEM((4, 4, TILE, TILE), BF16),
            pltpu.VMEM((2, D, D), BF16),
            pltpu.VMEM((FS, 16 * TILE), BF16),
            pltpu.VMEM((FS, 16 * TILE), BF16),
            pltpu.VMEM((OR, D), BF16),
            pltpu.VMEM((LAYERS + 1, NH, D, HR), BF16),
            pltpu.VMEM((LAYERS, D, 2 * D + 2 * AUX), BF16),
            pltpu.VMEM((CHIPS, 4, 4, TILE, TILE), BF16),
            pltpu.VMEM((CHIPS, 24, TILE), I32),
            pltpu.VMEM((2, CHIPS, TILE), I32),
            pltpu.VMEM((CHIPS, TILE), I32),
            pltpu.VMEM((CHIPS, 8, TILE), I32),
            pltpu.VMEM((CHIPS, 8, TILE), I32),
            pltpu.VMEM((LAYERS, NH, 2, CHIPS, FS, HR), BF16),
            pltpu.VMEM((2 * CHIPS, FS, ROWS), F32),
            pltpu.VMEM((LAYERS, NH, CHIPS, FS, HR), BF16),
            pltpu.VMEM((LAYERS, NH, CHIPS, FS, HR), BF16),
            pltpu.VMEM((LAYERS, ROWS, D), BF16),
            pltpu.VMEM((NH, D, HR), F32),
            pltpu.SMEM((CHIPS, 8, TILE), I32),
            dma((5,)), dma((OH,)), dma((OH,)), dma, dma,
            dma((48,)), dma((48,)),
            dma((LAYERS, NH)), dma((LAYERS, NH)),
            dma((LAYERS, NH)), dma((LAYERS, NH)),
            dma((LAYERS, NH)), dma((LAYERS, NH)),
            dma((LAYERS,)), dma((LAYERS,)),
            dma((LAYERS,)), dma((LAYERS,)),
            dma((LAYERS, OH)), dma((LAYERS, OH)),
            dma((CHIPS,)), dma((CHIPS,)),
            dma((CHIPS,)), dma((CHIPS,)),
            dma, dma,
        ],
        compiler_params=pltpu.CompilerParams(collective_id=0, has_side_effects=True, vmem_limit_bytes=60 << 20),
    )(features, send_rows, send_len, tile_src, tile_count, tile_val, w_self, w_neigh, gain, bias)


def solution(mesh):
    in_specs = (
        P(None, "dom", None),
        P(None, "dom", None, None),
        P(None, "dom", None),
        P(None, "dom", None),
        P(None, "dom"),
        P(None, "dom", None, None, None),
        P("segment", None, None),
        P("segment", None, None),
        P("segment", None),
        P("segment", None),
    )
    out_specs = P("segment", None, "dom", None)
    return jax.shard_map(
        per_device, mesh=mesh, in_specs=in_specs, out_specs=out_specs, check_vma=False
    )
```

```python
import jax
import jax.numpy as jnp
from jax import lax
from jax.experimental import pallas as pl
from jax.experimental.pallas import tpu as pltpu
from jax.sharding import PartitionSpec as P

norm_eps = 1e-05
MESH = pl.DeviceIdType.MESH
F32, BF16, I32 = jnp.float32, jnp.bfloat16, jnp.int32
LAYERS = 4
RING = 4
CHIPS = 16
GROUP = CHIPS // 2
TILE = 128
ROWS = 512
D = 512
FS = 32
AUX = 128
NH = 2
HR = ROWS // NH
BL = 4 // NH
OH = 2
OR = ROWS // OH


def kernel(
    feat_hbm, rows_ref, len_ref, src_ref, cnt_ref, tv_hbm, ws_hbm, wn_hbm, gain_ref, bias_ref,
    out_hbm,
    feat, tvs, w_in, ga, gb, relay, xt, wp, tv, meta, m1a, px, m1b, m1c, xc, xf, aggs, agg, outr, pre, qs,
    loc_sem, ol_sem, rl_s, rl_r, ro_s, tv_s, tv_r, t1_s, t1_r, fw_s, fw_r, t2_s, t2_r, w_s, w_r, wf_s, wf_r, o_s, o_r, m_s, m_r, mb_s, mb_r, pm_s, pm_r,
):
    x = lax.axis_index("segment")
    d = lax.axis_index("dom")
    k = lax.rem(d, 2)
    r = lax.div(d, 2)
    y, z = lax.div(r, RING), lax.rem(r, RING)

    def at_offset(dy, dz):
        return lax.rem(y + dy, RING) * RING + lax.rem(z + dz, RING)

    def to(o):
        return lax.rem(y + lax.div(o, RING), RING) * RING + lax.rem(z + lax.rem(o, RING), RING)

    def fro(o):
        return (
            lax.rem(y + RING - lax.div(o, RING), RING) * RING
            + lax.rem(z + RING - lax.rem(o, RING), RING)
        )

    def chip(c):
        return {"dom": c * 2 + k}

    partner = {"dom": r * 2 + (1 - k)}

    def seg(j):
        return {"segment": lax.rem(x + j, LAYERS)}

    def rcopy(src, dst, ssem, rsem, dev):
        return pltpu.make_async_remote_copy(
            src_ref=src, dst_ref=dst, send_sem=ssem, recv_sem=rsem, device_id=dev, device_id_type=MESH
        )

    def each(lo, hi, f):
        def body(i, c):
            f(i)
            return c
        lax.fori_loop(lo, hi, body, 0)

    load_f = pltpu.make_async_copy(feat_hbm.at[x], feat, loc_sem.at[0])
    load_t = pltpu.make_async_copy(tv_hbm.at[x], tvs, loc_sem.at[1])
    load_w = [pltpu.make_async_copy(src.at[0], w_in.at[e], loc_sem.at[3 + e]) for e, src in enumerate((ws_hbm, wn_hbm))]
    load_t.start()
    load_f.start()
    for copy in load_w:
        copy.start()

    barrier = pltpu.get_barrier_semaphore()
    each(1, CHIPS, lambda o: pl.semaphore_signal(barrier, inc=1, device_id=chip(to(o)), device_id_type=MESH))
    pl.semaphore_signal(barrier, inc=1, device_id=partner, device_id_type=MESH)
    for j in range(1, LAYERS):
        pl.semaphore_signal(barrier, inc=1, device_id=seg(j), device_id_type=MESH)

    def transpose_tiles(h):
        for i in range(2 * h, 2 * h + 2):
            for kk in range(4):
                tv[r, i, kk] = tvs[i, kk].astype(F32).T.astype(BF16)

    load_t.wait()
    transpose_tiles(0)
    pl.semaphore_wait(barrier, CHIPS - 1 + 1 + LAYERS - 1)

    counter = [0]

    def at(h, da, db, lo, n):
        yy, zz = (y + db, z + da) if h == 0 else (y + da, z + db)
        c = lax.rem(yy + 2 * RING, RING) * RING + lax.rem(zz + 2 * RING, RING)
        return tv.at[c, pl.ds(2 * h + lo, n)]

    def ring_send(h, first, da, db, s, lo, n):
        along_z = (h == 0) == first
        if along_z:
            dev = chip(y * RING + lax.rem(z + s + RING, RING))
        else:
            dev = chip(lax.rem(y + s + RING, RING) * RING + z)
        i = counter[0]
        counter[0] += 1
        ref = at(h, da, db, lo, n)
        c = rcopy(ref, ref, tv_s.at[i], tv_r.at[i], dev)
        c.start()
        return c, (h, da, db, lo, n, i)

    def ring_wait(entry, first, s):
        h, da, db, lo, n, i = entry[1]
        da, db = (da - s, db) if first else (da, db - s)
        ref = at(h, da, db, lo, n)
        rcopy(ref, ref, tv_s.at[i], tv_r.at[i], partner).wait_recv()

    s1, s1b, s2, s2b = {}, {}, {}, {}

    def second(h, da):
        for s in (1, -1):
            s2[h, da, s] = ring_send(h, False, da, 0, s, 0, 2)

    def second_fwd(h, da):
        for s in (1, -1):
            ring_wait(s2[h, da, s], False, s)
            s2b[h, da, s] = ring_send(h, False, da, -s, s, 0 if s == 1 else 1, 1)

    for h in range(2):
        if h == 1:
            transpose_tiles(1)
        for s in (1, -1):
            s1[h, s] = ring_send(h, True, 0, 0, s, 0, 2)
    load_f.wait()
    for b in range(D // TILE):
        for h in range(NH):
            part = feat[h * HR:(h + 1) * HR, b * TILE:(b + 1) * TILE]
            xt[0, h, b * TILE:(b + 1) * TILE, :] = part.astype(F32).T.astype(BF16)

    def t1_copy(l, h, dy, dz):
        c, g = at_offset(dy, dz), dy // 2
        return rcopy(
            xt.at[l, h, pl.ds(pl.multiple_of(c * FS, FS), FS)], xc.at[l, h, k, dy * RING + dz],
            t1_s.at[l, h, g], t1_r.at[l, h, g], chip(c),
        )

    def t1_all(l, h, g):
        lo = max(g * GROUP, 1)
        ref = xc.at[l, h, k, pl.ds(lo, (g + 1) * GROUP - lo)]
        return rcopy(ref, ref, t1_s.at[l, h, g], t1_r.at[l, h, g], partner)

    def fw_copy(l, h, g, kk):
        ref = xc.at[l, h, kk, pl.ds(g * GROUP, GROUP)]
        return rcopy(ref, ref, fw_s.at[l, h, g], fw_r.at[l, h, g], partner)

    def t1_start(l, h):
        for dy in (2, 3, 1, 0):
            for dz in (2, 3, 1, 0):
                if dy or dz:
                    t1_copy(l, h, dy, dz).start()
        xc[l, h, k, 0] = xt[l, h, pl.ds(pl.multiple_of(r * FS, FS), FS), :]

    def widen(l, h, g, kk):
        for o in range(g * GROUP, (g + 1) * GROUP):
            c = at_offset(RING - o // RING, RING - o % RING)
            xf[kk * CHIPS + c, :, h * HR:(h + 1) * HR] = xc[l, h, kk, o].astype(F32)

    def t1_finish(l):
        for h in range(NH):
            for g in range(2):
                t1_all(l, h, g).wait_recv()
                fw_copy(l, h, g, k).start()
                widen(l, h, g, k)
        for h in range(NH):
            for g in range(2):
                fw_copy(l, h, g, 1 - k).wait_recv()
                widen(l, h, g, 1 - k)

    for h in range(NH):
        t1_start(0, h)
    for h in range(2):
        second(h, 0)

    lane = lax.broadcasted_iota(I32, (1, TILE), 1)
    for p in range(2 * CHIPS):
        live = lane < len_ref[x, 0, p]
        m1a[p % 2, p // 2:p // 2 + 1, :] = jnp.where(live, rows_ref[x, 0, p:p + 1, :], -1)
    pm = rcopy(m1a.at[1 - k], px, pm_s, pm_r, partner)
    pm.start()

    for copy in load_w:
        copy.wait()
    for b in range(D // TILE):
        cols = slice(b * TILE, (b + 1) * TILE)
        wp[x, cols, 0:D] = w_in[0, :, cols].astype(F32).T.astype(BF16)
        wp[x, cols, D:2 * D] = w_in[1, :, cols].astype(F32).T.astype(BF16)
        wp[x, cols, 2 * D:2 * D + AUX] = jnp.broadcast_to(gain_ref[:, cols].astype(F32), (AUX, TILE)).T.astype(BF16)
        wp[x, cols, 2 * D + AUX:2 * D + 2 * AUX] = (
            jnp.broadcast_to(bias_ref[:, cols].astype(F32), (AUX, TILE)).T.astype(BF16)
        )

    def w_part(l, kk):
        return wp.at[l, pl.ds(pl.multiple_of(kk * (D // 2), D // 2), D // 2)]

    def w_copy(j):
        return rcopy(w_part(x, k), w_part(x, k), w_s.at[j], w_r.at[j], seg(j))

    def w_from(j):
        return lax.rem(x + LAYERS - j, LAYERS)

    def wf_copy(j, kk):
        ref = w_part(w_from(j), kk)
        return rcopy(ref, ref, wf_s.at[j], wf_r.at[j], partner)

    def w_forward(j):
        ref = w_part(w_from(j), k)
        rcopy(ref, ref, w_s.at[j], w_r.at[j], partner).wait_recv()
        wf_copy(j, k).start()

    for j in range(1, LAYERS):
        w_copy(j).start()

    pm.wait()
    m1b[...] = jnp.zeros(m1b.shape, I32)
    for c in range(CHIPS):
        m1b[c, pl.ds(k, 1), :] = m1a[k, c:c + 1, :]
        m1b[c, pl.ds(1 - k, 1), :] = px[c:c + 1, :]
    m1c[r] = m1b[r]

    def m1_copy(o):
        c = to(o)
        return rcopy(m1b.at[c], m1c.at[r], m_s.at[o], m_r.at[o], chip(c))

    each(1, CHIPS, lambda o: m1_copy(o).start())

    def gathered(q, idx):
        low = jnp.broadcast_to(idx & (TILE - 1), (FS, TILE))
        high = idx >> 7
        g = jnp.zeros((FS, TILE), F32)
        for b in range(ROWS // TILE):
            part = jnp.take_along_axis(xf[q, :, b * TILE:(b + 1) * TILE], low, axis=1)
            g = jnp.where(high == b, part, g)
        return g.astype(BF16)

    def t2_copy(l, h, c):
        return rcopy(aggs.at[l, h, c], agg.at[l, h, r], t2_s.at[l, h], t2_r.at[l, h], chip(c))

    def t2_all(l, h):
        ref = agg.at[l, h, pl.ds(0, CHIPS - 1)]
        return rcopy(ref, ref, t2_s.at[l, h], t2_r.at[l, h], partner)

    def gather(c, blocks, buf):
        for b, i in enumerate(blocks):
            for kk in range(4):
                t = 4 * i + kk
                buf[:, (4 * b + kk) * TILE:(4 * b + kk + 1) * TILE] = gathered(qs[c, 0, t], meta[c, t:t + 1, :])

    def multiply(l, c, blocks, buf, dst):
        for b, i in enumerate(blocks):
            a = jnp.dot(
                buf[:, 4 * b * TILE:4 * (b + 1) * TILE], tv[c, i].reshape(4 * TILE, TILE), preferred_element_type=F32
            )
            e = i % BL
            dst[l, i // BL, c, :, e * TILE:(e + 1) * TILE] = a.astype(BF16)

    def aggregate(l, h):
        blocks = range(h * BL, (h + 1) * BL)
        bufs = (ga, gb)
        gather(at_offset(RING - 1, RING - 1), blocks, ga)

        def row(dy, own):
            for n in range(RING):
                dz = RING - 1 - n
                c = at_offset(dy, dz)
                mine = own and dz == 0
                multiply(l, c, blocks, bufs[n % 2], agg if mine else aggs)
                if dz:
                    gather(at_offset(dy, dz - 1), blocks, bufs[(n + 1) % 2])
                elif not own:
                    gather(at_offset(dy - 1, RING - 1), blocks, ga)
                if not mine:
                    t2_copy(l, h, c).start()

        each(0, RING - 1, lambda t: row(RING - 1 - t, False))
        row(0, True)

    def out_rows(l, h):
        return outr.at[l, pl.ds(h * OR, OR)], out_hbm.at[0, x, pl.ds(h * OR, OR)]

    def out_local(l, h):
        src, dst = out_rows(l, h)
        return pltpu.make_async_copy(src, dst, ol_sem.at[h])

    def out_remote(l, h):
        j = lax.rem(x + LAYERS - l, LAYERS)
        src, dst = out_rows(l, h)
        return rcopy(src, dst, o_s.at[l, h], o_r.at[j, h], {"segment": l})

    last = LAYERS - 1

    def relay_in(l, e):
        src, _ = out_rows(l, e)
        via = lax.rem(l + (LAYERS - 1 if e == 0 else 1), LAYERS)
        return rcopy(src, relay, rl_s.at[e], rl_r, {"segment": via})

    def relay_out(l, e):
        return rcopy(relay, out_hbm.at[0, l - 2, pl.ds(e * OR, OR)], ro_s, o_r.at[2, e], {"segment": l})

    def pass_on(l, finish):
        for e, at_x in ((0, (l + 3) % LAYERS), (1, (l + 1) % LAYERS)):
            @pl.when(x == at_x)
            def _():
                if finish:
                    relay_out(l, e).wait_send()
                else:
                    relay_in(l, e).wait_recv()
                    relay_out(l, e).start()

    def by_place(l, local, remote, relayed):
        far = x == l - 2
        pl.when(x == l)(local)
        pl.when((x != l) & jnp.logical_not(far))(remote)
        pl.when(far)(relayed)

    def send_out(l, h):
        for b in range(D // TILE):
            part = xt[l + 1, h, b * TILE:(b + 1) * TILE, :]
            outr[l, h * HR:(h + 1) * HR, b * TILE:(b + 1) * TILE] = part.astype(F32).T.astype(BF16)
        halves = range(h * OH // NH, (h + 1) * OH // NH)

        def local():
            for e in halves:
                out_local(l, e).start()

        def remote():
            for e in halves:
                out_remote(l, e).start()

        def relayed():
            for e in halves:
                relay_in(l, e).start()

        by_place(l, local, remote, relayed)

    def dense(l, h):
        t2_all(l, h).wait_recv()
        rhs = agg[l, h].reshape(D, HR)
        v = pre[h] + jnp.dot(wp[l, :, D:2 * D], rhs, preferred_element_type=F32)
        pre[h] = v - jnp.mean(v, axis=0, keepdims=True)
        v = pre[h]
        scale = lax.rsqrt(jnp.mean(v * v, axis=0, keepdims=True) + norm_eps)
        g = wp[l, :, 2 * D:2 * D + AUX].astype(F32)
        b = wp[l, :, 2 * D + AUX:2 * D + 2 * AUX].astype(F32)
        for e in range(HR // AUX):
            cols = slice(e * AUX, (e + 1) * AUX)
            w = pre[h, :, cols] * scale[:, cols] * g + b
            xt[l + 1, h, :, cols] = jnp.maximum(w, 0.0).astype(BF16)

    def advance(l, h):
        @pl.when(l < last)
        def _():
            t1_start(l + 1, h)

        @pl.when(l == last)
        def _():
            send_out(l, h)

        if h == NH - 1:
            @pl.when(l < last)
            def _():
                for e in range(NH):
                    send_out(l, e)

    for h in range(2):
        for s in (1, -1):
            ring_wait(s1[h, s], True, s)
            s1b[h, s] = ring_send(h, True, -s, 0, s, 0 if s == 1 else 1, 1)
    for h in range(2):
        for s in (1, -1):
            second(h, -s)

    def m1_wait(o):
        rcopy(m1b.at[fro(o)], m1c.at[fro(o)], m_s.at[o], m_r.at[o], partner).wait_recv()
    each(1, CHIPS, m1_wait)

    picks = jnp.zeros((1, TILE), I32)
    for t in range(16):
        s = src_ref[x, t // 4, t % 4]
        q = jnp.maximum(s - 4, 0)
        row = m1c[q >> 1, pl.ds(q & 1, 1), :]
        row = jnp.where(s < 4, s * TILE + lane, row)
        row = jnp.where(t % 4 < cnt_ref[x, t // 4], row, -1)
        meta[r, t:t + 1, :] = row
        picks = jnp.where(lane == t, jnp.where(s < 4, k * CHIPS + r, (q & 1) * CHIPS + (q >> 1)), picks)
    meta[r, 16:24, :] = jnp.broadcast_to(picks, (8, TILE))

    def meta_copy(o, c, dev):
        return rcopy(meta.at[c], meta.at[c], mb_s.at[o], mb_r.at[o], dev)

    each(1, CHIPS, lambda o: meta_copy(o, r, chip(to(o))).start())

    for h in range(2):
        second_fwd(h, 0)
    for h in range(2):
        for s in (1, -1):
            ring_wait(s1b[h, s], True, s)
        second(h, 2)
    for da in (1, -1):
        for h in range(2):
            second_fwd(h, da)

    t1_finish(0)
    each(1, CHIPS, lambda o: meta_copy(o, fro(o), partner).wait_recv())
    move = pltpu.make_async_copy(meta.at[:, 16:24, :], qs, loc_sem.at[2])
    move.start()
    move.wait()

    def arrived(names):
        for name in names:
            ring_wait(s2b[name], False, name[2])

    order = [
        (0, 0), (0, 1), (0, -1), (1, 0), (-1, 0), (0, 2), (2, 0), (1, 1), (-1, -1), (1, -1), (-1, 1),
        (2, 1), (2, -1), (1, 2), (-1, 2), (2, 2),
    ]
    offsets = [(dy % RING, dz % RING) for dy, dz in order]
    bufs = (ga, gb)
    gather(at_offset(*offsets[0]), range(4), ga)

    def first_layer(lo, hi):
        for u in range(lo, hi):
            c = at_offset(*offsets[u])
            multiply(0, c, range(4), bufs[u % 2], aggs if u else agg)
            if u + 1 < CHIPS:
                gather(at_offset(*offsets[u + 1]), range(4), bufs[(u + 1) % 2])
            if u:
                for h in range(NH):
                    t2_copy(0, h, c).start()

    first_layer(0, 5)
    for h in range(2):
        second_fwd(h, 2)
    arrived([(h, 0, s) for h in range(2) for s in (1, -1)])
    first_layer(5, 11)
    for j in range(1, LAYERS):
        w_forward(j)
    arrived([(h, da, s) for da in (1, -1) for h in range(2) for s in (1, -1)])
    first_layer(11, 15)
    arrived([(h, 2, s) for h in range(2) for s in (1, -1)])
    first_layer(15, 16)

    def own_part(l):
        @pl.when(x != l)
        def _():
            j = lax.rem(x + LAYERS - l, LAYERS)
            wf_copy(j, 1 - k).wait_recv()

        for h in range(NH):
            pre[h] = jnp.dot(wp[l, :, 0:D], xt[l, h], preferred_element_type=F32)

    own_part(0)
    for h in range(NH):
        dense(0, h)
        advance(0, h)

    def layer(l):
        own_part(l)
        t1_finish(l)
        pl.when(l == last)(lambda: pass_on(last - 1, False))
        for h in range(NH):
            aggregate(l, h)
            if h > 0:
                dense(l, h - 1)
                advance(l, h - 1)
        dense(l, NH - 1)
        advance(l, NH - 1)

    each(1, LAYERS, layer)

    pass_on(last, False)

    for dct in (s1, s1b, s2, s2b):
        for c, _ in dct.values():
            c.wait_send()
    each(1, CHIPS, lambda o: m1_copy(o).wait_send())
    each(1, CHIPS, lambda o: meta_copy(o, r, chip(to(o))).wait_send())
    for j in range(1, LAYERS):
        w_copy(j).wait_send()
        wf_copy(j, k).wait_send()

    def sent(l):
        for h in range(NH):
            t2_all(l, h).wait_send()
            for g in range(2):
                t1_all(l, h, g).wait_send()
                fw_copy(l, h, g, k).wait_send()

        def local():
            for e in range(OH):
                out_local(l, e).wait()

        def remote():
            for e in range(OH):
                out_remote(l, e).wait_send()

        def relayed():
            for e in range(OH):
                relay_in(l, e).wait_send()

        by_place(l, local, remote, relayed)

    each(0, LAYERS, sent)
    pass_on(last - 1, True)
    pass_on(last, True)
    for j in range(1, LAYERS):
        c = lax.rem(x + j, LAYERS)
        for e in range(OH):
            src, _ = out_rows(0, e)
            rcopy(src, out_hbm.at[0, c, pl.ds(e * OR, OR)], o_s.at[0, e], o_r.at[j, e], partner).wait_recv()


def per_device(features, send_rows, send_len, tile_src, tile_count, tile_val, w_self, w_neigh, gain, bias):
    any_, vmem, smem = (pl.BlockSpec(memory_space=s) for s in (pl.ANY, pltpu.VMEM, pltpu.SMEM))
    dma = pltpu.SemaphoreType.DMA
    return pl.pallas_call(
        kernel,
        out_shape=jax.ShapeDtypeStruct((1, 4, ROWS, D), BF16),
        in_specs=[any_, vmem, smem, smem, smem, any_, any_, any_, vmem, vmem],
        out_specs=any_,
        scratch_shapes=[
            pltpu.VMEM((ROWS, D), BF16),
            pltpu.VMEM((4, 4, TILE, TILE), BF16),
            pltpu.VMEM((2, D, D), BF16),
            pltpu.VMEM((FS, 16 * TILE), BF16),
            pltpu.VMEM((FS, 16 * TILE), BF16),
            pltpu.VMEM((OR, D), BF16),
            pltpu.VMEM((LAYERS + 1, NH, D, HR), BF16),
            pltpu.VMEM((LAYERS, D, 2 * D + 2 * AUX), BF16),
            pltpu.VMEM((CHIPS, 4, 4, TILE, TILE), BF16),
            pltpu.VMEM((CHIPS, 24, TILE), I32),
            pltpu.VMEM((2, CHIPS, TILE), I32),
            pltpu.VMEM((CHIPS, TILE), I32),
            pltpu.VMEM((CHIPS, 8, TILE), I32),
            pltpu.VMEM((CHIPS, 8, TILE), I32),
            pltpu.VMEM((LAYERS, NH, 2, CHIPS, FS, HR), BF16),
            pltpu.VMEM((2 * CHIPS, FS, ROWS), F32),
            pltpu.VMEM((LAYERS, NH, CHIPS, FS, HR), BF16),
            pltpu.VMEM((LAYERS, NH, CHIPS, FS, HR), BF16),
            pltpu.VMEM((LAYERS, ROWS, D), BF16),
            pltpu.VMEM((NH, D, HR), F32),
            pltpu.SMEM((CHIPS, 8, TILE), I32),
            dma((5,)), dma((OH,)), dma((OH,)), dma, dma,
            dma((48,)), dma((48,)),
            dma((LAYERS, NH, 2)), dma((LAYERS, NH, 2)),
            dma((LAYERS, NH, 2)), dma((LAYERS, NH, 2)),
            dma((LAYERS, NH)), dma((LAYERS, NH)),
            dma((LAYERS,)), dma((LAYERS,)),
            dma((LAYERS,)), dma((LAYERS,)),
            dma((LAYERS, OH)), dma((LAYERS, OH)),
            dma((CHIPS,)), dma((CHIPS,)),
            dma((CHIPS,)), dma((CHIPS,)),
            dma, dma,
        ],
        compiler_params=pltpu.CompilerParams(collective_id=0, has_side_effects=True, vmem_limit_bytes=60 << 20),
    )(features, send_rows, send_len, tile_src, tile_count, tile_val, w_self, w_neigh, gain, bias)


def solution(mesh):
    in_specs = (
        P(None, "dom", None),
        P(None, "dom", None, None),
        P(None, "dom", None),
        P(None, "dom", None),
        P(None, "dom"),
        P(None, "dom", None, None, None),
        P("segment", None, None),
        P("segment", None, None),
        P("segment", None),
        P("segment", None),
    )
    out_specs = P("segment", None, "dom", None)
    return jax.shard_map(
        per_device, mesh=mesh, in_specs=in_specs, out_specs=out_specs, check_vma=False
    )
```

```python
import jax
import jax.numpy as jnp
from jax import lax
from jax.experimental import pallas as pl
from jax.experimental.pallas import tpu as pltpu
from jax.sharding import PartitionSpec as P

norm_eps = 1e-05
MESH = pl.DeviceIdType.MESH
F32, BF16, I32 = jnp.float32, jnp.bfloat16, jnp.int32
LAYERS = 4
RING = 4
CHIPS = 16
TILE = 128
ROWS = 512
D = 512
FS = 32
AUX = 128
NH = 2
HR = ROWS // NH
BL = 4 // NH
OH = 2
OR = ROWS // OH


def kernel(
    feat_hbm, rows_ref, len_ref, src_ref, cnt_ref, tv_hbm, ws_hbm, wn_hbm, gain_ref, bias_ref,
    out_hbm,
    feat, tvs, w_in, ga, gb, relay, xt, wp, tv, meta, m1a, px, m1b, m1c, xc, xf, aggs, agg, outr, pre, qs,
    loc_sem, ol_sem, rl_s, rl_r, ro_s, tv_s, tv_r, t1_s, t1_r, fw_s, fw_r, t2_s, t2_r, w_s, w_r, wf_s, wf_r, o_s, o_r, m_s, m_r, mb_s, mb_r, pm_s, pm_r,
):
    x = lax.axis_index("segment")
    d = lax.axis_index("dom")
    k = lax.rem(d, 2)
    r = lax.div(d, 2)
    y, z = lax.div(r, RING), lax.rem(r, RING)

    def at_offset(dy, dz):
        return lax.rem(y + dy, RING) * RING + lax.rem(z + dz, RING)

    def to(o):
        return lax.rem(y + lax.div(o, RING), RING) * RING + lax.rem(z + lax.rem(o, RING), RING)

    def fro(o):
        return (
            lax.rem(y + RING - lax.div(o, RING), RING) * RING
            + lax.rem(z + RING - lax.rem(o, RING), RING)
        )

    def chip(c):
        return {"dom": c * 2 + k}

    partner = {"dom": r * 2 + (1 - k)}

    def seg(j):
        return {"segment": lax.rem(x + j, LAYERS)}

    def rcopy(src, dst, ssem, rsem, dev):
        return pltpu.make_async_remote_copy(
            src_ref=src, dst_ref=dst, send_sem=ssem, recv_sem=rsem, device_id=dev, device_id_type=MESH
        )

    def each(lo, hi, f):
        def body(i, c):
            f(i)
            return c
        lax.fori_loop(lo, hi, body, 0)

    load_f = pltpu.make_async_copy(feat_hbm.at[x], feat, loc_sem.at[0])
    load_t = pltpu.make_async_copy(tv_hbm.at[x], tvs, loc_sem.at[1])
    load_w = [pltpu.make_async_copy(src.at[0], w_in.at[e], loc_sem.at[3 + e]) for e, src in enumerate((ws_hbm, wn_hbm))]
    load_t.start()
    load_f.start()
    for copy in load_w:
        copy.start()

    barrier = pltpu.get_barrier_semaphore()
    each(1, CHIPS, lambda o: pl.semaphore_signal(barrier, inc=1, device_id=chip(to(o)), device_id_type=MESH))
    pl.semaphore_signal(barrier, inc=1, device_id=partner, device_id_type=MESH)
    for j in range(1, LAYERS):
        pl.semaphore_signal(barrier, inc=1, device_id=seg(j), device_id_type=MESH)

    def transpose_tiles(h):
        for i in range(2 * h, 2 * h + 2):
            for kk in range(4):
                tv[r, i, kk] = tvs[i, kk].astype(F32).T.astype(BF16)

    load_t.wait()
    transpose_tiles(0)
    pl.semaphore_wait(barrier, CHIPS - 1 + 1 + LAYERS - 1)

    counter = [0]

    def at(h, da, db, lo, n):
        yy, zz = (y + db, z + da) if h == 0 else (y + da, z + db)
        c = lax.rem(yy + 2 * RING, RING) * RING + lax.rem(zz + 2 * RING, RING)
        return tv.at[c, pl.ds(2 * h + lo, n)]

    def ring_send(h, first, da, db, s, lo, n):
        along_z = (h == 0) == first
        if along_z:
            dev = chip(y * RING + lax.rem(z + s + RING, RING))
        else:
            dev = chip(lax.rem(y + s + RING, RING) * RING + z)
        i = counter[0]
        counter[0] += 1
        ref = at(h, da, db, lo, n)
        c = rcopy(ref, ref, tv_s.at[i], tv_r.at[i], dev)
        c.start()
        return c, (h, da, db, lo, n, i)

    def ring_wait(entry, first, s):
        h, da, db, lo, n, i = entry[1]
        da, db = (da - s, db) if first else (da, db - s)
        ref = at(h, da, db, lo, n)
        rcopy(ref, ref, tv_s.at[i], tv_r.at[i], partner).wait_recv()

    s1, s1b, s2, s2b = {}, {}, {}, {}

    def second(h, da):
        for s in (1, -1):
            s2[h, da, s] = ring_send(h, False, da, 0, s, 0, 2)

    def second_fwd(h, da):
        for s in (1, -1):
            ring_wait(s2[h, da, s], False, s)
            s2b[h, da, s] = ring_send(h, False, da, -s, s, 0 if s == 1 else 1, 1)

    for h in range(2):
        if h == 1:
            transpose_tiles(1)
        for s in (1, -1):
            s1[h, s] = ring_send(h, True, 0, 0, s, 0, 2)
    load_f.wait()
    for b in range(D // TILE):
        for h in range(NH):
            part = feat[h * HR:(h + 1) * HR, b * TILE:(b + 1) * TILE]
            xt[0, h, b * TILE:(b + 1) * TILE, :] = part.astype(F32).T.astype(BF16)

    def t1_copy(l, h, c):
        return rcopy(
            xt.at[l, h, pl.ds(pl.multiple_of(c * FS, FS), FS)], xc.at[l, h, k, r], t1_s.at[l, h], t1_r.at[l, h], chip(c)
        )

    def t1_all(l, h):
        ref = xc.at[l, h, k, pl.ds(0, CHIPS - 1)]
        return rcopy(ref, ref, t1_s.at[l, h], t1_r.at[l, h], partner)

    def fw_copy(l, h, kk):
        ref = xc.at[l, h, kk]
        return rcopy(ref, ref, fw_s.at[l, h], fw_r.at[l, h], partner)

    def t1_start(l, h):
        for dy in (2, 3, 1, 0):
            for dz in (2, 3, 1, 0):
                if dy or dz:
                    t1_copy(l, h, at_offset(dy, dz)).start()
        xc[l, h, k, r] = xt[l, h, pl.ds(pl.multiple_of(r * FS, FS), FS), :]

    def widen(l, h, kk):
        def four(g):
            for e in range(RING):
                c = g * RING + e
                xf[kk * CHIPS + c, :, h * HR:(h + 1) * HR] = xc[l, h, kk, c].astype(F32)
        each(0, CHIPS // RING, four)

    def t1_finish(l):
        for h in range(NH):
            t1_all(l, h).wait_recv()
            fw_copy(l, h, k).start()
            widen(l, h, k)
            fw_copy(l, h, 1 - k).wait_recv()
            widen(l, h, 1 - k)

    for h in range(NH):
        t1_start(0, h)
    for h in range(2):
        second(h, 0)

    lane = lax.broadcasted_iota(I32, (1, TILE), 1)
    for p in range(2 * CHIPS):
        live = lane < len_ref[x, 0, p]
        m1a[p % 2, p // 2:p // 2 + 1, :] = jnp.where(live, rows_ref[x, 0, p:p + 1, :], -1)
    pm = rcopy(m1a.at[1 - k], px, pm_s, pm_r, partner)
    pm.start()

    for copy in load_w:
        copy.wait()
    for b in range(D // TILE):
        cols = slice(b * TILE, (b + 1) * TILE)
        wp[x, cols, 0:D] = w_in[0, :, cols].astype(F32).T.astype(BF16)
        wp[x, cols, D:2 * D] = w_in[1, :, cols].astype(F32).T.astype(BF16)
        wp[x, cols, 2 * D:2 * D + AUX] = jnp.broadcast_to(gain_ref[:, cols].astype(F32), (AUX, TILE)).T.astype(BF16)
        wp[x, cols, 2 * D + AUX:2 * D + 2 * AUX] = (
            jnp.broadcast_to(bias_ref[:, cols].astype(F32), (AUX, TILE)).T.astype(BF16)
        )

    def w_part(l, kk):
        return wp.at[l, pl.ds(pl.multiple_of(kk * (D // 2), D // 2), D // 2)]

    def w_copy(j):
        return rcopy(w_part(x, k), w_part(x, k), w_s.at[j], w_r.at[j], seg(j))

    def w_from(j):
        return lax.rem(x + LAYERS - j, LAYERS)

    def wf_copy(j, kk):
        ref = w_part(w_from(j), kk)
        return rcopy(ref, ref, wf_s.at[j], wf_r.at[j], partner)

    def w_forward(j):
        ref = w_part(w_from(j), k)
        rcopy(ref, ref, w_s.at[j], w_r.at[j], partner).wait_recv()
        wf_copy(j, k).start()

    for j in range(1, LAYERS):
        w_copy(j).start()

    pm.wait()
    m1b[...] = jnp.zeros(m1b.shape, I32)
    for c in range(CHIPS):
        m1b[c, pl.ds(k, 1), :] = m1a[k, c:c + 1, :]
        m1b[c, pl.ds(1 - k, 1), :] = px[c:c + 1, :]
    m1c[r] = m1b[r]

    def m1_copy(o):
        c = to(o)
        return rcopy(m1b.at[c], m1c.at[r], m_s.at[o], m_r.at[o], chip(c))

    each(1, CHIPS, lambda o: m1_copy(o).start())

    def gathered(q, idx):
        low = jnp.broadcast_to(idx & (TILE - 1), (FS, TILE))
        high = idx >> 7
        g = jnp.zeros((FS, TILE), F32)
        for b in range(ROWS // TILE):
            part = jnp.take_along_axis(xf[q, :, b * TILE:(b + 1) * TILE], low, axis=1)
            g = jnp.where(high == b, part, g)
        return g.astype(BF16)

    def t2_copy(l, h, c):
        return rcopy(aggs.at[l, h, c], agg.at[l, h, r], t2_s.at[l, h], t2_r.at[l, h], chip(c))

    def t2_all(l, h):
        ref = agg.at[l, h, pl.ds(0, CHIPS - 1)]
        return rcopy(ref, ref, t2_s.at[l, h], t2_r.at[l, h], partner)

    def gather(c, blocks, buf):
        for b, i in enumerate(blocks):
            for kk in range(4):
                t = 4 * i + kk
                buf[:, (4 * b + kk) * TILE:(4 * b + kk + 1) * TILE] = gathered(qs[c, 0, t], meta[c, t:t + 1, :])

    def multiply(l, c, blocks, buf, dst):
        for b, i in enumerate(blocks):
            a = jnp.dot(
                buf[:, 4 * b * TILE:4 * (b + 1) * TILE], tv[c, i].reshape(4 * TILE, TILE), preferred_element_type=F32
            )
            e = i % BL
            dst[l, i // BL, c, :, e * TILE:(e + 1) * TILE] = a.astype(BF16)

    def aggregate(l, h):
        blocks = range(h * BL, (h + 1) * BL)
        bufs = (ga, gb)
        gather(at_offset(RING - 1, RING - 1), blocks, ga)

        def row(dy, own):
            for n in range(RING):
                dz = RING - 1 - n
                c = at_offset(dy, dz)
                mine = own and dz == 0
                multiply(l, c, blocks, bufs[n % 2], agg if mine else aggs)
                if dz:
                    gather(at_offset(dy, dz - 1), blocks, bufs[(n + 1) % 2])
                elif not own:
                    gather(at_offset(dy - 1, RING - 1), blocks, ga)
                if not mine:
                    t2_copy(l, h, c).start()

        each(0, RING - 1, lambda t: row(RING - 1 - t, False))
        row(0, True)

    def out_rows(l, h):
        return outr.at[l, pl.ds(h * OR, OR)], out_hbm.at[0, x, pl.ds(h * OR, OR)]

    def out_local(l, h):
        src, dst = out_rows(l, h)
        return pltpu.make_async_copy(src, dst, ol_sem.at[h])

    def out_remote(l, h):
        j = lax.rem(x + LAYERS - l, LAYERS)
        src, dst = out_rows(l, h)
        return rcopy(src, dst, o_s.at[l, h], o_r.at[j, h], {"segment": l})

    last = LAYERS - 1

    def relay_in(l, e):
        src, _ = out_rows(l, e)
        via = lax.rem(l + (LAYERS - 1 if e == 0 else 1), LAYERS)
        return rcopy(src, relay, rl_s.at[e], rl_r, {"segment": via})

    def relay_out(l, e):
        return rcopy(relay, out_hbm.at[0, l - 2, pl.ds(e * OR, OR)], ro_s, o_r.at[2, e], {"segment": l})

    def pass_on(l, finish):
        for e, at_x in ((0, (l + 3) % LAYERS), (1, (l + 1) % LAYERS)):
            @pl.when(x == at_x)
            def _():
                if finish:
                    relay_out(l, e).wait_send()
                else:
                    relay_in(l, e).wait_recv()
                    relay_out(l, e).start()

    def by_place(l, local, remote, relayed):
        far = x == l - 2
        pl.when(x == l)(local)
        pl.when((x != l) & jnp.logical_not(far))(remote)
        pl.when(far)(relayed)

    def send_out(l, h):
        for b in range(D // TILE):
            part = xt[l + 1, h, b * TILE:(b + 1) * TILE, :]
            outr[l, h * HR:(h + 1) * HR, b * TILE:(b + 1) * TILE] = part.astype(F32).T.astype(BF16)
        halves = range(h * OH // NH, (h + 1) * OH // NH)

        def local():
            for e in halves:
                out_local(l, e).start()

        def remote():
            for e in halves:
                out_remote(l, e).start()

        def relayed():
            for e in halves:
                relay_in(l, e).start()

        by_place(l, local, remote, relayed)

    def dense(l, h):
        t2_all(l, h).wait_recv()
        rhs = agg[l, h].reshape(D, HR)
        v = pre[h] + jnp.dot(wp[l, :, D:2 * D], rhs, preferred_element_type=F32)
        pre[h] = v - jnp.mean(v, axis=0, keepdims=True)
        v = pre[h]
        scale = lax.rsqrt(jnp.mean(v * v, axis=0, keepdims=True) + norm_eps)
        g = wp[l, :, 2 * D:2 * D + AUX].astype(F32)
        b = wp[l, :, 2 * D + AUX:2 * D + 2 * AUX].astype(F32)
        for e in range(HR // AUX):
            cols = slice(e * AUX, (e + 1) * AUX)
            w = pre[h, :, cols] * scale[:, cols] * g + b
            xt[l + 1, h, :, cols] = jnp.maximum(w, 0.0).astype(BF16)

    def advance(l, h):
        @pl.when(l < last)
        def _():
            t1_start(l + 1, h)

        @pl.when(l == last)
        def _():
            send_out(l, h)

        if h == NH - 1:
            @pl.when(l < last)
            def _():
                for e in range(NH):
                    send_out(l, e)

    for h in range(2):
        for s in (1, -1):
            ring_wait(s1[h, s], True, s)
            s1b[h, s] = ring_send(h, True, -s, 0, s, 0 if s == 1 else 1, 1)
    for h in range(2):
        for s in (1, -1):
            second(h, -s)

    def m1_wait(o):
        rcopy(m1b.at[fro(o)], m1c.at[fro(o)], m_s.at[o], m_r.at[o], partner).wait_recv()
    each(1, CHIPS, m1_wait)

    picks = jnp.zeros((1, TILE), I32)
    for t in range(16):
        s = src_ref[x, t // 4, t % 4]
        q = jnp.maximum(s - 4, 0)
        row = m1c[q >> 1, pl.ds(q & 1, 1), :]
        row = jnp.where(s < 4, s * TILE + lane, row)
        row = jnp.where(t % 4 < cnt_ref[x, t // 4], row, -1)
        meta[r, t:t + 1, :] = row
        picks = jnp.where(lane == t, jnp.where(s < 4, k * CHIPS + r, (q & 1) * CHIPS + (q >> 1)), picks)
    meta[r, 16:24, :] = jnp.broadcast_to(picks, (8, TILE))

    def meta_copy(o, c, dev):
        return rcopy(meta.at[c], meta.at[c], mb_s.at[o], mb_r.at[o], dev)

    each(1, CHIPS, lambda o: meta_copy(o, r, chip(to(o))).start())

    for h in range(2):
        second_fwd(h, 0)
    for h in range(2):
        for s in (1, -1):
            ring_wait(s1b[h, s], True, s)
        second(h, 2)
    for da in (1, -1):
        for h in range(2):
            second_fwd(h, da)

    t1_finish(0)
    each(1, CHIPS, lambda o: meta_copy(o, fro(o), partner).wait_recv())
    move = pltpu.make_async_copy(meta.at[:, 16:24, :], qs, loc_sem.at[2])
    move.start()
    move.wait()

    def arrived(names):
        for name in names:
            ring_wait(s2b[name], False, name[2])

    order = [
        (0, 0), (0, 1), (0, -1), (1, 0), (-1, 0), (0, 2), (2, 0), (1, 1), (-1, -1), (1, -1), (-1, 1),
        (2, 1), (2, -1), (1, 2), (-1, 2), (2, 2),
    ]
    offsets = [(dy % RING, dz % RING) for dy, dz in order]
    bufs = (ga, gb)
    gather(at_offset(*offsets[0]), range(4), ga)

    def first_layer(lo, hi):
        for u in range(lo, hi):
            c = at_offset(*offsets[u])
            multiply(0, c, range(4), bufs[u % 2], aggs if u else agg)
            if u + 1 < CHIPS:
                gather(at_offset(*offsets[u + 1]), range(4), bufs[(u + 1) % 2])
            if u:
                for h in range(NH):
                    t2_copy(0, h, c).start()

    first_layer(0, 5)
    for h in range(2):
        second_fwd(h, 2)
    arrived([(h, 0, s) for h in range(2) for s in (1, -1)])
    first_layer(5, 11)
    for j in range(1, LAYERS):
        w_forward(j)
    arrived([(h, da, s) for da in (1, -1) for h in range(2) for s in (1, -1)])
    first_layer(11, 15)
    arrived([(h, 2, s) for h in range(2) for s in (1, -1)])
    first_layer(15, 16)

    def own_part(l):
        @pl.when(x != l)
        def _():
            j = lax.rem(x + LAYERS - l, LAYERS)
            wf_copy(j, 1 - k).wait_recv()

        for h in range(NH):
            pre[h] = jnp.dot(wp[l, :, 0:D], xt[l, h], preferred_element_type=F32)

    own_part(0)
    for h in range(NH):
        dense(0, h)
        advance(0, h)

    def layer(l):
        own_part(l)
        t1_finish(l)
        pl.when(l == last)(lambda: pass_on(last - 1, False))
        for h in range(NH):
            aggregate(l, h)
            if h > 0:
                dense(l, h - 1)
                advance(l, h - 1)
        dense(l, NH - 1)
        advance(l, NH - 1)

    each(1, LAYERS, layer)

    pass_on(last, False)

    for dct in (s1, s1b, s2, s2b):
        for c, _ in dct.values():
            c.wait_send()
    each(1, CHIPS, lambda o: m1_copy(o).wait_send())
    each(1, CHIPS, lambda o: meta_copy(o, r, chip(to(o))).wait_send())
    for j in range(1, LAYERS):
        w_copy(j).wait_send()
        wf_copy(j, k).wait_send()

    def sent(l):
        for h in range(NH):
            t1_all(l, h).wait_send()
            t2_all(l, h).wait_send()
            fw_copy(l, h, k).wait_send()

        def local():
            for e in range(OH):
                out_local(l, e).wait()

        def remote():
            for e in range(OH):
                out_remote(l, e).wait_send()

        def relayed():
            for e in range(OH):
                relay_in(l, e).wait_send()

        by_place(l, local, remote, relayed)

    each(0, LAYERS, sent)
    pass_on(last - 1, True)
    pass_on(last, True)
    for j in range(1, LAYERS):
        c = lax.rem(x + j, LAYERS)
        for e in range(OH):
            src, _ = out_rows(0, e)
            rcopy(src, out_hbm.at[0, c, pl.ds(e * OR, OR)], o_s.at[0, e], o_r.at[j, e], partner).wait_recv()


def per_device(features, send_rows, send_len, tile_src, tile_count, tile_val, w_self, w_neigh, gain, bias):
    any_, vmem, smem = (pl.BlockSpec(memory_space=s) for s in (pl.ANY, pltpu.VMEM, pltpu.SMEM))
    dma = pltpu.SemaphoreType.DMA
    return pl.pallas_call(
        kernel,
        out_shape=jax.ShapeDtypeStruct((1, 4, ROWS, D), BF16),
        in_specs=[any_, vmem, smem, smem, smem, any_, any_, any_, vmem, vmem],
        out_specs=any_,
        scratch_shapes=[
            pltpu.VMEM((ROWS, D), BF16),
            pltpu.VMEM((4, 4, TILE, TILE), BF16),
            pltpu.VMEM((2, D, D), BF16),
            pltpu.VMEM((FS, 16 * TILE), BF16),
            pltpu.VMEM((FS, 16 * TILE), BF16),
            pltpu.VMEM((OR, D), BF16),
            pltpu.VMEM((LAYERS + 1, NH, D, HR), BF16),
            pltpu.VMEM((LAYERS, D, 2 * D + 2 * AUX), BF16),
            pltpu.VMEM((CHIPS, 4, 4, TILE, TILE), BF16),
            pltpu.VMEM((CHIPS, 24, TILE), I32),
            pltpu.VMEM((2, CHIPS, TILE), I32),
            pltpu.VMEM((CHIPS, TILE), I32),
            pltpu.VMEM((CHIPS, 8, TILE), I32),
            pltpu.VMEM((CHIPS, 8, TILE), I32),
            pltpu.VMEM((LAYERS, NH, 2, CHIPS, FS, HR), BF16),
            pltpu.VMEM((2 * CHIPS, FS, ROWS), F32),
            pltpu.VMEM((LAYERS, NH, CHIPS, FS, HR), BF16),
            pltpu.VMEM((LAYERS, NH, CHIPS, FS, HR), BF16),
            pltpu.VMEM((LAYERS, ROWS, D), BF16),
            pltpu.VMEM((NH, D, HR), F32),
            pltpu.SMEM((CHIPS, 8, TILE), I32),
            dma((5,)), dma((OH,)), dma((OH,)), dma, dma,
            dma((48,)), dma((48,)),
            dma((LAYERS, NH)), dma((LAYERS, NH)),
            dma((LAYERS, NH)), dma((LAYERS, NH)),
            dma((LAYERS, NH)), dma((LAYERS, NH)),
            dma((LAYERS,)), dma((LAYERS,)),
            dma((LAYERS,)), dma((LAYERS,)),
            dma((LAYERS, OH)), dma((LAYERS, OH)),
            dma((CHIPS,)), dma((CHIPS,)),
            dma((CHIPS,)), dma((CHIPS,)),
            dma, dma,
        ],
        compiler_params=pltpu.CompilerParams(collective_id=0, has_side_effects=True, vmem_limit_bytes=60 << 20),
    )(features, send_rows, send_len, tile_src, tile_count, tile_val, w_self, w_neigh, gain, bias)


def solution(mesh):
    in_specs = (
        P(None, "dom", None),
        P(None, "dom", None, None),
        P(None, "dom", None),
        P(None, "dom", None),
        P(None, "dom"),
        P(None, "dom", None, None, None),
        P("segment", None, None),
        P("segment", None, None),
        P("segment", None),
        P("segment", None),
    )
    out_specs = P("segment", None, "dom", None)
    return jax.shard_map(
        per_device, mesh=mesh, in_specs=in_specs, out_specs=out_specs, check_vma=False
    )
```
